1024 devices in a mesh: plan: 128 (over z, y, core), height: 8 (over x).
Axes of the slice: x: 8, y: 8, z: 8, core: 2. Of those that a mesh axis runs over, the one named last changes fastest.
Arguments:
- right_side: float32 [128, 8, 64, 128], P('plan', 'height'), may hold values from -6 to 6
- couplings: bfloat16 [128, 8, 3, 64, 64, 128], P('plan', 'height'), may hold values from -0.3125 to 0.3125
- neighbours: int32 [128, 8, 3, 128], P('plan', 'height'), may hold values from 0 to 639
- aggregates: int32 [128, 8, 128], P('plan', 'height'), may hold values from 0 to 15
- coarse_ops: bfloat16 [64, 64, 160], replicated, may hold values from -0.5 to 2
- coarse_smooth: bfloat16 [64, 64, 176], replicated, may hold values from -0.5 to 2
Outputs:
- solution: float32 [128, 8, 64, 128], P('plan', 'height')
The draws below stay inside these ranges and needn't reach their ends.
All inputs are finite; a program needn't handle non-finite values.
Results may differ from the reference program's by a relative error of at most 0.0003.
Values sent between devices are 32-bit elements; how exact they have to be, the bound alone decides.
No kernel may reach another device: no remote copies, remote signals or barrier semaphores. Data moves between devices by JAX's collectives and lax.ppermute only.
A program may use at most 128 MiB of HBM per device.

```python
import math
import jax
import jax.numpy as jnp
from jax import lax

BS = 64
NB = 128
NC = 16
LEVELS = 10
N_PLAN = 128
N_HEIGHT = 8


def draw_coarse_ops(key, part):
    width = LEVELS * NC
    noise_key = jax.random.fold_in(key, 11)
    diag_key = jax.random.fold_in(key, 12)
    noise = jax.random.truncated_normal(noise_key, -3.0, 3.0, (BS, BS, width), jnp.float32) * (0.4 / math.sqrt(BS))
    diagonal = jax.random.uniform(diag_key, (BS, width), jnp.float32, 0.8, 1.3)
    identity = jnp.eye(BS, dtype=jnp.float32)[:, :, None]
    return (noise + identity * diagonal[None, :, :]).astype(jnp.bfloat16)


def draw_coarse_smooth(key, part):
    width = (LEVELS + 1) * NC
    noise_key = jax.random.fold_in(key, 21)
    small_key = jax.random.fold_in(key, 22)
    large_key = jax.random.fold_in(key, 23)
    coarsest = jnp.arange(width) >= LEVELS * NC
    spread = jnp.where(coarsest, 0.3, 0.04) / math.sqrt(BS)
    noise = jax.random.truncated_normal(noise_key, -3.0, 3.0, (BS, BS, width), jnp.float32) * spread[None, None, :]
    small_diag = jax.random.uniform(small_key, (BS, width), jnp.float32, 0.08, 0.16)
    large_diag = jax.random.uniform(large_key, (BS, width), jnp.float32, 0.7, 1.3)
    diagonal = jnp.where(coarsest[None, :], large_diag, small_diag)
    identity = jnp.eye(BS, dtype=jnp.float32)[:, :, None]
    return (noise + identity * diagonal[None, :, :]).astype(jnp.bfloat16)


def touch_ends(result, rng, low, top_value):
    spot = [jax.random.randint(jax.random.fold_in(rng, axis), (), 0, length) for axis, length in enumerate(result.shape)]
    widest = result.shape.index(max(result.shape))
    beside = spot[:widest] + [(spot[widest] + 1) % result.shape[widest]] + spot[widest + 1:]
    return result.at[tuple(spot)].set(low).at[tuple(beside)].set(top_value)


def shard_levels(rng, extent, cuts, least, top_value):
    gain, own = 1.0, jax.random.fold_in(rng, 6)
    for dim, shards_of in cuts:
        heights = jnp.exp(jax.random.uniform(jax.random.fold_in(own, dim), (shards_of,), jnp.float32, least / len(cuts), top_value / len(cuts)))
        gain = gain * jnp.repeat(heights, extent[dim] // shards_of).reshape([-1 if axis == dim else 1 for axis in range(len(extent))])
    return gain


def normal_values(key, shape, scale, reach, cuts=(), held_as=jnp.bfloat16):
    values = jax.random.normal(key, shape, jnp.float32) * scale
    if len(cuts) > 0:
        values = shard_levels(key, shape, cuts, -0.22, 0.18) * values
    return jnp.clip(values, min=-reach, max=reach).astype(held_as)


def setup_inputs(seed: int = 0) -> dict:
    seeds = jax.random.split(jax.random.key(seed), 7)
    return {
        "right_side": normal_values(seeds[0], (N_PLAN, N_HEIGHT, BS, NB), 1.0, 6.0, ((0, 128), (1, 8)), jnp.float32),
        "couplings": normal_values(seeds[1], (N_PLAN, N_HEIGHT, 3, BS, BS, NB), (5 * BS) ** -0.5, 0.3125, ((0, 128), (1, 8))),
        "neighbours": touch_ends(jax.random.randint(seeds[2], (N_PLAN, N_HEIGHT, 3, NB), 0, 5 * NB), jax.random.fold_in(seeds[2], 1), 0, (5 * NB) - 1).astype(jnp.int32),
        "aggregates": touch_ends(jax.random.randint(seeds[3], (N_PLAN, N_HEIGHT, NB), 0, NC), jax.random.fold_in(seeds[3], 1), 0, NC - 1).astype(jnp.int32),
        "coarse_ops": draw_coarse_ops(jax.random.fold_in(seeds[6], 71), 0),
        "coarse_smooth": draw_coarse_smooth(jax.random.fold_in(seeds[6], 71), 0),
    }


HALF_ROOT = 0.7071067811865476
OMEGA = 0.5

def couple(weights, vector):
    return jnp.einsum('ijc,...jc->...ic', weights.astype(jnp.float32), vector.astype(jnp.float32), precision=lax.Precision.HIGHEST)

def couple_fine(weights, vector):
    return jnp.einsum('...ijb,...jb->...ib', weights.astype(jnp.float32), vector.astype(jnp.float32), precision=lax.Precision.HIGHEST)

def extend_field(field):
    zero_layer = jnp.zeros_like(field[:, :1])
    below = jnp.concatenate([zero_layer, field[:, :-1]], axis=1)
    above = jnp.concatenate([field[:, 1:], zero_layer], axis=1)
    zero_row = jnp.zeros_like(field[:1])
    before = jnp.concatenate([zero_row, field[:-1]], axis=0)
    after = jnp.concatenate([field[1:], zero_row], axis=0)
    return jnp.concatenate([field, below, above, before, after], axis=3)

def apply_fine(field, couplings, neighbours):
    extended = extend_field(field)

    def plan_row(pieces):
        field_row, extended_row, coupling_row, link_row = pieces
        summed = field_row
        for which in range(3):
            columns = jnp.broadcast_to(link_row[:, which, None, :], field_row.shape)
            picked = jnp.take_along_axis(extended_row, columns, axis=2)
            summed = summed + couple_fine(coupling_row[:, which], picked)
        return summed
    return lax.map(plan_row, (field, extended, couplings, neighbours))

def reference(right_side, couplings, neighbours, aggregates, coarse_ops, coarse_smooth):
    first = OMEGA * right_side
    second = first + OMEGA * (right_side - apply_fine(first, couplings, neighbours))
    residual = right_side - apply_fine(second, couplings, neighbours)
    member = (aggregates[..., None] == jnp.arange(NC, dtype=jnp.int32)).astype(jnp.float32)
    level_rhs = jnp.einsum('phib,phbc->phic', residual, member, precision=lax.Precision.HIGHEST) * math.sqrt(NC / NB)
    groups = jnp.transpose(level_rhs, (1, 0, 2, 3)).reshape(N_HEIGHT * N_PLAN, BS, NC)
    saved = []
    for level in range(LEVELS):
        operator = coarse_ops[:, :, level * NC:(level + 1) * NC]
        smoother = coarse_smooth[:, :, level * NC:(level + 1) * NC]
        smoothed = couple(smoother, groups)
        remain = groups - couple(operator, smoothed)
        saved.append((groups, smoothed))
        paired = remain.reshape(-1, 2, BS, NC)
        groups = (paired[:, 0] + paired[:, 1]) * HALF_ROOT
    correction = couple(coarse_smooth[:, :, LEVELS * NC:], groups)
    for level in reversed(range(LEVELS)):
        operator = coarse_ops[:, :, level * NC:(level + 1) * NC]
        smoother = coarse_smooth[:, :, level * NC:(level + 1) * NC]
        level_groups, smoothed = saved[level]
        halves = jnp.repeat(correction, 2, axis=0)
        correction = smoothed + halves
        correction = correction + couple(smoother, level_groups - couple(operator, correction))
    fine_correction = jnp.transpose(correction.reshape(N_HEIGHT, N_PLAN, BS, NC), (1, 0, 2, 3))
    third = second + jnp.einsum('phic,phbc->phib', fine_correction, member, precision=lax.Precision.HIGHEST)
    return third + OMEGA * (right_side - apply_fine(third, couplings, neighbours))
```

```python
import functools
import math

import jax
import jax.numpy as jnp
from jax import lax
from jax.experimental import pallas as pl
from jax.experimental.pallas import tpu as pltpu
from jax.sharding import PartitionSpec as P

BS = 64
NB = 128
NC = 16
LEVELS = 10
SUB = 8
GROUPS = BS // SUB
F32 = jnp.float32
MIB = 1 << 20


def whole(count):
    return [pl.BlockSpec(memory_space=pltpu.VMEM)] * count


def call(body, out_shape, inputs, limit, scratch=()):
    several = isinstance(out_shape, (tuple, list))
    return pl.pallas_call(
        body,
        out_shape=out_shape,
        in_specs=whole(len(inputs)),
        out_specs=whole(len(out_shape)) if several else whole(1)[0],
        scratch_shapes=scratch,
        compiler_params=pltpu.CompilerParams(vmem_limit_bytes=limit),
    )(*inputs)


def iota(shape, axis):
    return lax.broadcasted_iota(jnp.int32, shape, axis)


def fold(rows):
    sub = iota((SUB, NB), 0)
    step = 1
    while len(rows) > 1:
        keep = (sub & step) == 0
        rows = [
            jnp.where(keep, a, b) + pltpu.roll(jnp.where(keep, b, a), step, 0)
            for a, b in zip(rows[0::2], rows[1::2])
        ]
        step *= 2
    return rows[0]


def take_lanes(value, index):
    return jnp.take_along_axis(value, index, axis=1, mode="promise_in_bounds")


def pick(fields, links_ref):
    picked = []
    for which in range(3):
        link = jnp.broadcast_to(links_ref[which : which + 1, :], (BS, NB))
        lane, part = link & (NB - 1), link >> 7
        value = take_lanes(fields[0], lane)
        for number in range(1, 5):
            value = jnp.where(part == number, take_lanes(fields[number], lane), value)
        picked.append(value)
    return picked


def coupled(weights_ref, picked, tile):
    rows = []
    for row in range(SUB):
        total = None
        for which in range(3):
            product = weights_ref[which, tile * SUB + row].astype(F32) * picked[which]
            for part in range(GROUPS):
                piece = product[part * SUB : (part + 1) * SUB]
                total = piece if total is None else total + piece
        rows.append(total)
    return fold(rows)


def tiles(step):
    def body(tile, carry):
        step(tile, pl.ds(pl.multiple_of(tile * SUB, SUB), SUB))
        return carry

    lax.fori_loop(0, GROUPS, body, 0)


def first_body(source, below, above, before, after, weights, links, second):
    fields = [ref[...] for ref in (source, below, above, before, after)]
    picked = pick(fields, links)

    def step(tile, rows):
        mine = source[rows, :]
        applied = 0.5 * (mine + coupled(weights, picked, tile))
        second[rows, :] = 0.5 * mine + 0.5 * (mine - applied)

    tiles(step)


def second_body(field, below, above, before, after, weights, links, source, owners, sent, left):
    fields = [ref[...] for ref in (field, below, above, before, after)]
    picked = pick(fields, links)

    def step(tile, rows):
        left[rows, :] = source[rows, :] - (field[rows, :] + coupled(weights, picked, tile))

    tiles(step)
    member = ((iota((NB, NB), 0) & (NC - 1)) == owners[...]).astype(F32)
    spread = lax.dot_general(
        left[...],
        member,
        (((1,), (1,)), ((), ())),
        precision=lax.Precision.HIGHEST,
        preferred_element_type=F32,
    )
    lane_group = iota((SUB, NB), 1) // NC
    packed = spread[0:SUB]
    for group in range(1, GROUPS):
        packed = jnp.where(lane_group == group, spread[group * SUB : (group + 1) * SUB], packed)
    packed = packed * math.sqrt(NC / NB)
    for copy in range(sent.shape[0]):
        sent[copy] = packed


def last_body(field, below, above, before, after, weights, links, source, out):
    fields = [ref[...] for ref in (field, below, above, before, after)]
    picked = pick(fields, links)

    def step(tile, rows):
        mine = field[rows, :]
        applied = mine + coupled(weights, picked, tile)
        out[rows, :] = mine + 0.5 * (source[rows, :] - applied)

    tiles(step)


def swap_blocks(values):
    group = iota((SUB, NB), 1) // NC
    values = list(values)
    for bit in (1, 2, 4):
        keep = (group & bit) == 0
        for low in range(8):
            if low & bit:
                continue
            a, b = values[low], values[low | bit]
            values[low] = jnp.where(keep, a, pltpu.roll(b, NC * bit, 1))
            values[low | bit] = jnp.where(keep, pltpu.roll(a, NB - NC * bit, 1), b)
    return values


def pack_body(ops, smooth, packed, ops_high, smooth_high):
    lane = iota((SUB, NB), 1)

    def body(number, carry):
        inner = number
        low_ops, low_smooth, high = [], [], []
        for part in range(GROUPS):
            row = part * SUB + inner
            low_ops.append(ops[row, :, 0:NB].astype(F32))
            low_smooth.append(smooth[row, :, 0:NB].astype(F32))
            ops_high[part, :, 0 : 2 * NC] = ops[row, :, NB:].astype(F32)
            smooth_high[part, :, 0 : 3 * NC] = smooth[row, :, NB:].astype(F32)
        for column in range(GROUPS):
            rows = slice(column * SUB, (column + 1) * SUB)
            place = column * SUB + inner
            for level, value in enumerate(swap_blocks([v[rows] for v in low_ops])):
                packed[level, place] = value
            for level, value in enumerate(swap_blocks([v[rows] for v in low_smooth])):
                packed[LEVELS + level, place] = value
            high = [
                jnp.where(
                    lane < 2 * NC,
                    ops_high[part, rows, :],
                    pltpu.roll(smooth_high[part, rows, :], 2 * NC, 1),
                )
                for part in range(GROUPS)
            ]
            high = swap_blocks(high)
            for level, place_of in enumerate((8, 9, LEVELS + 8, LEVELS + 9, LEVELS + 10)):
                packed[place_of, place] = high[level]
        return carry

    lax.fori_loop(0, SUB, body, 0)


def block_product(packed, number, vectors):
    lane = iota((SUB, NB), 1) & (NC - 1)
    totals = [[None] * SUB for _ in vectors]
    for column in range(GROUPS):
        spread = [take_lanes(v, lane + column * NC) for v in vectors]
        for row in range(SUB):
            weight = packed[number, column * SUB + row]
            for total, value in zip(totals, spread):
                piece = weight * value
                total[row] = piece if total[row] is None else total[row] + piece
    return [fold(total) for total in totals]


def climb(packed, first_level, received, me, kept, sent):
    count = received.shape[0].bit_length() - 1
    columns = [received[me]]
    for bits in range(1, count + 1):
        start = (me >> bits) << bits
        total = received[start]
        for other in range(1, 2**bits):
            total = total + received[start + other]
        columns.append(total * 2.0 ** (-bits / 2))
    for step in range(count):
        level = first_level + step
        smoothed = block_product(packed, LEVELS + level, columns)
        kept[2 * step] = columns[0]
        kept[2 * step + 1] = smoothed[0]
        removed = block_product(packed, level, smoothed[1:])
        columns = [a - b for a, b in zip(columns[1:], removed)]
    return columns[0]


def climb_body(first_level, axis, shift, packed, received, sent, kept):
    me = (lax.axis_index(axis) >> shift) & (received.shape[0] - 1)
    top = climb(packed, first_level, received, me, kept, sent)
    for copy in range(sent.shape[0]):
        sent[copy] = top


def turn_body(axis, packed, received, low, middle, field, owners, third, kept):
    first_level = LEVELS - (received.shape[0].bit_length() - 1)
    top = climb(packed, first_level, received, lax.axis_index(axis), kept, None)
    (error,) = block_product(packed, 2 * LEVELS, [top])
    low_levels = low.shape[0] // 2
    for level in reversed(range(LEVELS)):
        if level >= first_level:
            saved, place = kept, level - first_level
        elif level >= low_levels:
            saved, place = middle, level - low_levels
        else:
            saved, place = low, level
        error = saved[2 * place + 1] + error
        (applied,) = block_product(packed, level, [error])
        (fixed,) = block_product(packed, LEVELS + level, [saved[2 * place] - applied])
        error = error + fixed
    owner = jnp.broadcast_to(owners[...], (SUB, NB))
    for group in range(GROUPS):
        rows = slice(group * SUB, (group + 1) * SUB)
        third[rows, :] = field[rows, :] + take_lanes(error, owner + group * NC)


def shifted(value, axis, step):
    count = lax.axis_size(axis)
    pairs = [(i, i + step) for i in range(count) if 0 <= i + step < count]
    return lax.ppermute(value, axis, pairs)


def halo(value):
    return (
        shifted(value, "height", 1),
        shifted(value, "height", -1),
        shifted(value, "plan", 1),
        shifted(value, "plan", -1),
    )


def exchange(value, axis, groups=None):
    return lax.all_to_all(value, axis, 0, 0, axis_index_groups=groups, tiled=True)


def shards(right_side, couplings, neighbours, aggregates, coarse_ops, coarse_smooth):
    source = right_side[0, 0]
    weights = couplings[0, 0]
    links = neighbours[0, 0]
    owners = aggregates[0]
    plan = lax.axis_size("plan")
    height = lax.axis_size("height")
    height_bits = height.bit_length() - 1
    plan_bits = plan.bit_length() - 1
    low_bits = (plan_bits + 1) // 2
    near = 2**low_bits
    far = plan // near
    field_shape = jax.ShapeDtypeStruct((BS, NB), F32)

    def vectors(count):
        return jax.ShapeDtypeStruct((count, SUB, NB), F32)

    packed = call(
        pack_body,
        jax.ShapeDtypeStruct((2 * LEVELS + 1, BS, SUB, NB), F32),
        (coarse_ops, coarse_smooth),
        24 * MIB,
        [pltpu.VMEM((GROUPS, BS, NB), F32)] * 2,
    )
    second = call(
        first_body, field_shape, (source, *halo(source), weights, links), 12 * MIB
    )
    sent = call(
        second_body,
        vectors(near),
        (second, *halo(second), weights, links, source, owners),
        12 * MIB,
        [pltpu.VMEM((BS, NB), F32)],
    )
    near_groups = [[a * near + b for b in range(near)] for a in range(far)]
    far_groups = [[a * near + b for a in range(far)] for b in range(near)]
    received = exchange(sent, "plan", near_groups)
    sent, low = call(
        functools.partial(climb_body, 0, "plan", 0),
        (vectors(far), vectors(2 * low_bits)),
        (packed, received),
        16 * MIB,
    )
    received = exchange(sent, "plan", far_groups)
    sent, middle = call(
        functools.partial(climb_body, low_bits, "plan", low_bits),
        (vectors(height), vectors(2 * (plan_bits - low_bits))),
        (packed, received),
        16 * MIB,
    )
    received = exchange(sent, "height")
    third = call(
        functools.partial(turn_body, "height"),
        field_shape,
        (packed, received, low, middle, second, owners),
        16 * MIB,
        [pltpu.VMEM((2 * height_bits, SUB, NB), F32)],
    )
    out = call(
        last_body, field_shape, (third, *halo(third), weights, links, source), 12 * MIB
    )
    return out[None, None]


def solution(mesh):
    in_specs = (
        P("plan", "height", None, None),
        P("plan", "height", None, None, None, None),
        P("plan", "height", None, None),
        P("plan", "height", None),
        P(),
        P(),
    )
    out_specs = P("plan", "height", None, None)
    return jax.shard_map(shards, mesh=mesh, in_specs=in_specs, out_specs=out_specs, check_vma=False)
```

```python
import math

import jax
import jax.numpy as jnp
from jax import lax
from jax.experimental import pallas as pl
from jax.experimental.pallas import tpu as pltpu
from jax.sharding import PartitionSpec as P

BS = 64
NB = 128
NC = 16
LEVELS = 10
SUB = 8
GROUPS = BS // SUB
F32 = jnp.float32
MIB = 1 << 20


def whole(count):
    return [pl.BlockSpec(memory_space=pltpu.VMEM)] * count


def call(body, out_shape, inputs, limit, scratch=()):
    several = isinstance(out_shape, (tuple, list))
    return pl.pallas_call(
        body,
        out_shape=out_shape,
        in_specs=whole(len(inputs)),
        out_specs=whole(len(out_shape)) if several else whole(1)[0],
        scratch_shapes=scratch,
        compiler_params=pltpu.CompilerParams(vmem_limit_bytes=limit),
    )(*inputs)


def iota(shape, axis):
    return lax.broadcasted_iota(jnp.int32, shape, axis)


def fold(rows):
    sub = iota((SUB, NB), 0)
    step = 1
    while len(rows) > 1:
        keep = (sub & step) == 0
        rows = [
            jnp.where(keep, a, b) + pltpu.roll(jnp.where(keep, b, a), step, 0)
            for a, b in zip(rows[0::2], rows[1::2])
        ]
        step *= 2
    return rows[0]


def take_lanes(value, index):
    return jnp.take_along_axis(value, index, axis=1, mode="promise_in_bounds")


def pick(fields, links_ref):
    picked = []
    for which in range(3):
        link = jnp.broadcast_to(links_ref[which], (BS, NB))
        lane, part = link & (NB - 1), link >> 7
        value = take_lanes(fields[0], lane)
        for number in range(1, 5):
            value = jnp.where(part == number, take_lanes(fields[number], lane), value)
        picked.append(value)
    return picked


def coupled(weights_ref, picked, tile):
    rows = []
    for row in range(SUB):
        total = None
        for which in range(3):
            product = weights_ref[which, tile * SUB + row].astype(F32) * picked[which]
            for part in range(GROUPS):
                piece = product[part * SUB : (part + 1) * SUB]
                total = piece if total is None else total + piece
        rows.append(total)
    return fold(rows)


def tiles(step):
    def body(tile, carry):
        step(tile, pl.ds(pl.multiple_of(tile * SUB, SUB), SUB))
        return carry

    lax.fori_loop(0, GROUPS, body, 0)


def first_body(source, below, above, before, after, weights, links, second):
    fields = [ref[...] for ref in (source, below, above, before, after)]
    picked = pick(fields, links)

    def step(tile, rows):
        mine = source[rows, :]
        applied = 0.5 * (mine + coupled(weights, picked, tile))
        second[rows, :] = 0.5 * mine + 0.5 * (mine - applied)

    tiles(step)


def second_body(field, below, above, before, after, weights, links, source, owners, sent, left):
    fields = [ref[...] for ref in (field, below, above, before, after)]
    picked = pick(fields, links)

    def step(tile, rows):
        left[rows, :] = source[rows, :] - (field[rows, :] + coupled(weights, picked, tile))

    tiles(step)
    member = ((iota((NB, NB), 0) & (NC - 1)) == owners[...]).astype(F32)
    spread = lax.dot_general(
        left[...],
        member,
        (((1,), (1,)), ((), ())),
        precision=lax.Precision.HIGHEST,
        preferred_element_type=F32,
    )
    lane_group = iota((SUB, NB), 1) // NC
    packed = spread[0:SUB]
    for group in range(1, GROUPS):
        packed = jnp.where(lane_group == group, spread[group * SUB : (group + 1) * SUB], packed)
    packed = packed * math.sqrt(NC / NB)
    for copy in range(sent.shape[0]):
        sent[copy] = packed


def last_body(field, below, above, before, after, weights, links, source, out):
    fields = [ref[...] for ref in (field, below, above, before, after)]
    picked = pick(fields, links)

    def step(tile, rows):
        mine = field[rows, :]
        applied = mine + coupled(weights, picked, tile)
        out[rows, :] = mine + 0.5 * (source[rows, :] - applied)

    tiles(step)


def skew(values, count):
    group = iota((SUB, NB), 1) // NC
    values = [v if g == 0 else pltpu.roll(v, NC * g, 1) for g, v in enumerate(values)]
    wanted = [(GROUPS - level) % GROUPS for level in range(count)]
    needed = [set(wanted)]
    for bit in (4, 2):
        needed.append({v for v in needed[-1]} | {(v + bit) % GROUPS for v in needed[-1]})
    for bit, places in zip((1, 2, 4), reversed(needed)):
        second = (group & bit) != 0
        values = [
            jnp.where(second, values[(v + bit) % GROUPS], values[v]) if v in places else None
            for v in range(GROUPS)
        ]
    return [values[v] for v in wanted]


def pack_body(ops, smooth, packed, ops_high, smooth_high):
    def body(inner, carry):
        for part in range(GROUPS):
            row = part * SUB + inner
            ops_high[part, :, 0 : 2 * NC] = ops[row, :, NB:].astype(F32)
            smooth_high[part, :, 0 : 3 * NC] = smooth[row, :, NB:].astype(F32)
        for column in range(GROUPS):
            rows = slice(column * SUB, (column + 1) * SUB)
            place = column * SUB + inner
            for base, low, high, count in (
                (0, ops, ops_high, 2),
                (LEVELS, smooth, smooth_high, 3),
            ):
                values = [low[part * SUB + inner, rows, 0:NB].astype(F32) for part in range(GROUPS)]
                for level, value in enumerate(skew(values, GROUPS)):
                    packed[base + level, place] = value
                values = [high[part, rows, :] for part in range(GROUPS)]
                for level, value in enumerate(skew(values, count)):
                    packed[base + GROUPS + level, place] = value
        return carry

    lax.fori_loop(0, SUB, body, 0)


def block_product(packed, number, vectors, turned):
    lane = iota((SUB, NB), 1) & (NC - 1)
    totals = [[None] * SUB for _ in vectors]
    for column in range(GROUPS):
        place = lane + ((column + turned) % GROUPS) * NC
        spread = [take_lanes(v, place) for v in vectors]
        for row in range(SUB):
            weight = packed[number, column * SUB + row]
            for total, value in zip(totals, spread):
                piece = weight * value
                total[row] = piece if total[row] is None else total[row] + piece
    return [fold(total) for total in totals]


def climb(packed, first_level, received, me, kept):
    count = received.shape[0].bit_length() - 1
    columns = [received[me]]
    for bits in range(1, count + 1):
        start = (me >> bits) << bits
        total = received[start]
        for other in range(1, 2**bits):
            total = total + received[start + other]
        columns.append(total * 2.0 ** (-bits / 2))
    for step in range(count):
        level = first_level + step
        smoothed = block_product(packed, LEVELS + level, columns, max(level - 1, 0))
        if level > 0:
            columns = [pltpu.roll(v, NC, 1) for v in columns]
        kept[2 * step] = columns[0]
        kept[2 * step + 1] = smoothed[0]
        removed = block_product(packed, level, smoothed[1:], level)
        columns = [a - b for a, b in zip(columns[1:], removed)]
    return columns[0]


def climb_body(packed, received, sent, kept):
    me = lax.axis_index("plan") & (received.shape[0] - 1)
    top = climb(packed, 0, received, me, kept)
    for copy in range(sent.shape[0]):
        sent[copy] = top


def turn_body(packed, received, low, field, owners, third, kept):
    low_levels = low.shape[0] // 2
    near = 2**low_levels
    far = lax.axis_size("plan") // near
    me = lax.axis_index("height") * far + lax.axis_index("plan") // near
    top = climb(packed, low_levels, received, me, kept)
    (error,) = block_product(packed, 2 * LEVELS, [top], LEVELS - 1)
    for level in reversed(range(LEVELS)):
        saved, place = (low, level) if level < low_levels else (kept, level - low_levels)
        error = pltpu.roll(saved[2 * place + 1], NC, 1) + error
        (applied,) = block_product(packed, level, [error], level + 1)
        (fixed,) = block_product(packed, LEVELS + level, [saved[2 * place] - applied], level)
        error = pltpu.roll(error, NB - NC, 1) + fixed
    owner = jnp.broadcast_to(owners[...], (SUB, NB))
    for group in range(GROUPS):
        rows = slice(group * SUB, (group + 1) * SUB)
        third[rows, :] = field[rows, :] + take_lanes(error, owner + group * NC)


def shifted(value, axis, step):
    count = lax.axis_size(axis)
    pairs = [(i, i + step) for i in range(count) if 0 <= i + step < count]
    return lax.ppermute(value, axis, pairs)


def halo(value):
    return (
        shifted(value, "height", 1),
        shifted(value, "height", -1),
        shifted(value, "plan", 1),
        shifted(value, "plan", -1),
    )


def exchange(value, axis, groups=None):
    return lax.all_to_all(value, axis, 0, 0, axis_index_groups=groups, tiled=True)


def shards(right_side, couplings, neighbours, aggregates, coarse_ops, coarse_smooth):
    source = right_side[0, 0]
    weights = couplings[0, 0]
    links = neighbours[0, 0][:, None, :]
    owners = aggregates[0]
    plan = lax.axis_size("plan")
    height = lax.axis_size("height")
    plan_bits = plan.bit_length() - 1
    low_bits = (plan_bits + 1) // 2
    near = 2**low_bits
    far = plan // near
    field_shape = jax.ShapeDtypeStruct((BS, NB), F32)

    def vectors(count):
        return jax.ShapeDtypeStruct((count, SUB, NB), F32)

    packed = call(
        pack_body,
        jax.ShapeDtypeStruct((2 * LEVELS + 1, BS, SUB, NB), F32),
        (coarse_ops, coarse_smooth),
        24 * MIB,
        [pltpu.VMEM((GROUPS, BS, NB), F32)] * 2,
    )
    around = halo(source)
    packed, source = lax.optimization_barrier((packed, source))
    second = call(first_body, field_shape, (source, *around, weights, links), 12 * MIB)
    sent = call(
        second_body,
        vectors(near),
        (second, *halo(second), weights, links, source, owners),
        12 * MIB,
        [pltpu.VMEM((BS, NB), F32)],
    )
    near_groups = [[a * near + b for b in range(near)] for a in range(far)]
    received = exchange(sent, "plan", near_groups)
    sent, low = call(
        climb_body, (vectors(far * height), vectors(2 * low_bits)), (packed, received), 16 * MIB
    )
    far_groups = [
        [(a * near + b) * height + h for h in range(height) for a in range(far)]
        for b in range(near)
    ]
    received = exchange(sent, ("plan", "height"), far_groups)
    third = call(
        turn_body,
        field_shape,
        (packed, received, low, second, owners),
        16 * MIB,
        [pltpu.VMEM((2 * (LEVELS - low_bits), SUB, NB), F32)],
    )
    out = call(
        last_body, field_shape, (third, *halo(third), weights, links, source), 12 * MIB
    )
    return out[None, None]


def solution(mesh):
    in_specs = (
        P("plan", "height", None, None),
        P("plan", "height", None, None, None, None),
        P("plan", "height", None, None),
        P("plan", "height", None),
        P(),
        P(),
    )
    out_specs = P("plan", "height", None, None)
    return jax.shard_map(shards, mesh=mesh, in_specs=in_specs, out_specs=out_specs, check_vma=False)
```

```python
import functools
import math

import jax
import jax.numpy as jnp
from jax import lax
from jax.experimental import pallas as pl
from jax.experimental.pallas import tpu as pltpu
from jax.sharding import PartitionSpec as P

BS = 64
NB = 128
NC = 16
LEVELS = 10
SUB = 8
GROUPS = BS // SUB
F32 = jnp.float32
MIB = 1 << 20


def whole(count):
    return [pl.BlockSpec(memory_space=pltpu.VMEM)] * count


def call(body, out_shape, inputs, limit, scratch=()):
    several = isinstance(out_shape, (tuple, list))
    return pl.pallas_call(
        body,
        out_shape=out_shape,
        in_specs=whole(len(inputs)),
        out_specs=whole(len(out_shape)) if several else whole(1)[0],
        scratch_shapes=scratch,
        compiler_params=pltpu.CompilerParams(vmem_limit_bytes=limit),
    )(*inputs)


def iota(shape, axis):
    return lax.broadcasted_iota(jnp.int32, shape, axis)


def fold(rows):
    sub = iota((SUB, NB), 0)
    step = 1
    while len(rows) > 1:
        keep = (sub & step) == 0
        rows = [
            jnp.where(keep, a, b) + pltpu.roll(jnp.where(keep, b, a), step, 0)
            for a, b in zip(rows[0::2], rows[1::2])
        ]
        step *= 2
    return rows[0]


def take_lanes(value, index):
    return jnp.take_along_axis(value, index, axis=1, mode="promise_in_bounds")


def pick(fields, links_ref):
    odd = lax.axis_index("plan") & 1
    numbers = (0, 4 - odd, 3 + odd, 2, 1)
    picked = []
    for which in range(3):
        link = jnp.broadcast_to(links_ref[which], (BS, NB))
        lane, part = link & (NB - 1), link >> 7
        value = take_lanes(fields[0], lane)
        for number, field in zip(numbers[1:], fields[1:]):
            value = jnp.where(part == number, take_lanes(field, lane), value)
        picked.append(value)
    return picked


def coupled(weights_ref, picked, tile):
    rows = []
    for row in range(SUB):
        total = None
        for which in range(3):
            product = weights_ref[which, tile * SUB + row].astype(F32) * picked[which]
            for part in range(GROUPS):
                piece = product[part * SUB : (part + 1) * SUB]
                total = piece if total is None else total + piece
        rows.append(total)
    return fold(rows)


def tiles(step):
    def body(tile, carry):
        step(tile, pl.ds(pl.multiple_of(tile * SUB, SUB), SUB))
        return carry

    lax.fori_loop(0, GROUPS, body, 0)


def first_body(source, inner, outer, above, below, weights, links, second):
    fields = [ref[...] for ref in (source, inner, outer, above, below)]
    picked = pick(fields, links)

    def step(tile, rows):
        mine = source[rows, :]
        applied = 0.5 * (mine + coupled(weights, picked, tile))
        second[rows, :] = 0.5 * mine + 0.5 * (mine - applied)

    tiles(step)


def second_body(field, inner, outer, above, below, weights, links, source, owners, sent, left):
    fields = [ref[...] for ref in (field, inner, outer, above, below)]
    picked = pick(fields, links)

    def step(tile, rows):
        left[rows, :] = source[rows, :] - (field[rows, :] + coupled(weights, picked, tile))

    tiles(step)
    member = ((iota((NB, NB), 0) & (NC - 1)) == owners[...]).astype(F32)
    spread = lax.dot_general(
        left[...],
        member,
        (((1,), (1,)), ((), ())),
        precision=lax.Precision.HIGHEST,
        preferred_element_type=F32,
    )
    lane_group = iota((SUB, NB), 1) // NC
    packed = spread[0:SUB]
    for group in range(1, GROUPS):
        packed = jnp.where(lane_group == group, spread[group * SUB : (group + 1) * SUB], packed)
    packed = packed * math.sqrt(NC / NB)
    for copy in range(sent.shape[0]):
        sent[copy] = packed


def last_body(field, inner, outer, above, below, weights, links, source, out):
    fields = [ref[...] for ref in (field, inner, outer, above, below)]
    picked = pick(fields, links)

    def step(tile, rows):
        mine = field[rows, :]
        applied = mine + coupled(weights, picked, tile)
        out[rows, :] = mine + 0.5 * (source[rows, :] - applied)

    tiles(step)


def skew(values, count):
    group = iota((SUB, NB), 1) // NC
    values = [v if g == 0 else pltpu.roll(v, NC * g, 1) for g, v in enumerate(values)]
    wanted = [(GROUPS - level) % GROUPS for level in range(count)]
    needed = [set(wanted)]
    for bit in (4, 2):
        needed.append({v for v in needed[-1]} | {(v + bit) % GROUPS for v in needed[-1]})
    for bit, places in zip((1, 2, 4), reversed(needed)):
        second = (group & bit) != 0
        values = [
            jnp.where(second, values[(v + bit) % GROUPS], values[v]) if v in places else None
            for v in range(GROUPS)
        ]
    return [values[v] for v in wanted]


def pack_body(source, packed, high):
    count = packed.shape[0]
    rest = (count - GROUPS) * NC

    def body(inner, carry):
        for part in range(GROUPS):
            high[part, :, 0:rest] = source[part, inner, :, NB:].astype(F32)
        for column in range(GROUPS):
            rows = slice(column * SUB, (column + 1) * SUB)
            place = column * SUB + inner
            values = [source[part, inner, rows, 0:NB].astype(F32) for part in range(GROUPS)]
            for level, value in enumerate(skew(values, GROUPS)):
                packed[level, place] = value
            values = [high[part, rows, :] for part in range(GROUPS)]
            for level, value in enumerate(skew(values, count - GROUPS)):
                packed[GROUPS + level, place] = value
        return carry

    lax.fori_loop(0, SUB, body, 0)


def pack(blocks):
    width = blocks.shape[2]
    return call(
        pack_body,
        jax.ShapeDtypeStruct((width // NC, BS, SUB, NB), F32),
        (blocks.reshape(GROUPS, SUB, BS, width),),
        12 * MIB,
        [pltpu.VMEM((GROUPS, BS, NB), F32)],
    )


def block_product(packed, level, vectors, turned):
    lane = iota((SUB, NB), 1) & (NC - 1)
    totals = [[None] * SUB for _ in vectors]
    for column in range(GROUPS):
        place = lane + ((column + turned) % GROUPS) * NC
        spread = [take_lanes(v, place) for v in vectors]
        for row in range(SUB):
            weight = packed[level, column * SUB + row]
            for total, value in zip(totals, spread):
                piece = weight * value
                total[row] = piece if total[row] is None else total[row] + piece
    return [fold(total) for total in totals]


def climb(ops, smooth, first_level, received, me, kept):
    count = received.shape[0].bit_length() - 1
    columns = [received[me]]
    for bits in range(1, count + 1):
        start = (me >> bits) << bits
        total = received[start]
        for other in range(1, 2**bits):
            total = total + received[start + other]
        columns.append(total * 2.0 ** (-bits / 2))
    for step in range(count):
        level = first_level + step
        smoothed = block_product(smooth, level, columns, max(level - 1, 0))
        if level > 0:
            columns = [pltpu.roll(v, NC, 1) for v in columns]
        kept[2 * step] = columns[0]
        kept[2 * step + 1] = smoothed[0]
        removed = block_product(ops, level, smoothed[1:], level)
        columns = [a - b for a, b in zip(columns[1:], removed)]
    return columns[0]


def climb_body(first_level, ops, smooth, received, sent, kept):
    me = (lax.axis_index("plan") >> first_level) & (received.shape[0] - 1)
    top = climb(ops, smooth, first_level, received, me, kept)
    for copy in range(sent.shape[0]):
        sent[copy] = top


def turn_body(ops, smooth, received, low, middle, field, owners, third, high):
    levels = [
        (saved, 2 * place)
        for saved in (low, middle, high)
        for place in range(saved.shape[0] // 2)
    ]
    top = climb(ops, smooth, (low.shape[0] + middle.shape[0]) // 2, received, lax.axis_index("height"), high)
    (error,) = block_product(smooth, LEVELS, [top], LEVELS - 1)
    for level in reversed(range(LEVELS)):
        saved, place = levels[level]
        error = pltpu.roll(saved[place + 1], NC, 1) + error
        (applied,) = block_product(ops, level, [error], level + 1)
        (fixed,) = block_product(smooth, level, [saved[place] - applied], level)
        error = pltpu.roll(error, NB - NC, 1) + fixed
    owner = jnp.broadcast_to(owners[...], (SUB, NB))
    for group in range(GROUPS):
        rows = slice(group * SUB, (group + 1) * SUB)
        third[rows, :] = field[rows, :] + take_lanes(error, owner + group * NC)


def shifted(value, step):
    count = lax.axis_size("height")
    pairs = [(i, i + step) for i in range(count) if 0 <= i + step < count]
    return lax.ppermute(value, "height", pairs)


def swapped(value, first):
    pairs = []
    for low in range(first, lax.axis_size("plan") - 1, 2):
        pairs += [(low, low + 1), (low + 1, low)]
    return lax.ppermute(value, "plan", pairs)


def halo(value):
    inner, outer = swapped(value, 0), swapped(value, 1)
    above, below = shifted(value, -1), shifted(value, 1)
    return inner, outer, above, below


def exchange(value, axis, groups=None):
    return lax.all_to_all(value, axis, 0, 0, axis_index_groups=groups, tiled=True)


def shards(right_side, couplings, neighbours, aggregates, coarse_ops, coarse_smooth):
    source = right_side[0, 0]
    weights = couplings[0, 0]
    links = neighbours[0, 0][:, None, :]
    owners = aggregates[0]
    plan = lax.axis_size("plan")
    height = lax.axis_size("height")
    plan_bits = plan.bit_length() - 1
    low_bits = (plan_bits + 1) // 2
    near = 2**low_bits
    far = plan // near
    field_shape = jax.ShapeDtypeStruct((BS, NB), F32)

    def vectors(count):
        return jax.ShapeDtypeStruct((count, SUB, NB), F32)

    smooth = pack(coarse_smooth)
    around = halo(source)
    smooth, source = lax.optimization_barrier((smooth, source))
    second = call(first_body, field_shape, (source, *around, weights, links), 12 * MIB)
    around = halo(second)
    second, coarse_ops = lax.optimization_barrier((second, coarse_ops))
    ops = pack(coarse_ops)
    ops, source = lax.optimization_barrier((ops, source))
    sent = call(
        second_body,
        vectors(near),
        (second, *around, weights, links, source, owners),
        12 * MIB,
        [pltpu.VMEM((BS, NB), F32)],
    )
    near_groups = [[a * near + b for b in range(near)] for a in range(far)]
    far_groups = [[a * near + b for a in range(far)] for b in range(near)]
    received = exchange(sent, "plan", near_groups)
    sent, low = call(
        functools.partial(climb_body, 0),
        (vectors(far), vectors(2 * low_bits)),
        (ops, smooth, received),
        16 * MIB,
    )
    received = exchange(sent, "plan", far_groups)
    sent, middle = call(
        functools.partial(climb_body, low_bits),
        (vectors(height), vectors(2 * (plan_bits - low_bits))),
        (ops, smooth, received),
        16 * MIB,
    )
    received = exchange(sent, "height")
    third = call(
        turn_body,
        field_shape,
        (ops, smooth, received, low, middle, second, owners),
        16 * MIB,
        [pltpu.VMEM((2 * (LEVELS - plan_bits), SUB, NB), F32)],
    )
    out = call(
        last_body, field_shape, (third, *halo(third), weights, links, source), 12 * MIB
    )
    return out[None, None]


def solution(mesh):
    in_specs = (
        P("plan", "height", None, None),
        P("plan", "height", None, None, None, None),
        P("plan", "height", None, None),
        P("plan", "height", None),
        P(),
        P(),
    )
    out_specs = P("plan", "height", None, None)
    return jax.shard_map(shards, mesh=mesh, in_specs=in_specs, out_specs=out_specs, check_vma=False)
```

```python
import functools
import math

import jax
import jax.numpy as jnp
from jax import lax
from jax.experimental import pallas as pl
from jax.experimental.pallas import tpu as pltpu
from jax.sharding import PartitionSpec as P

BS = 64
NB = 128
NC = 16
LEVELS = 10
SUB = 8
GROUPS = BS // SUB
F32 = jnp.float32
MIB = 1 << 20
HALF_ROOT = 0.7071067811865476
BATCH = 4


def whole(count):
    return [pl.BlockSpec(memory_space=pltpu.VMEM)] * count


def call(body, out_shape, inputs, limit, scratch=()):
    several = isinstance(out_shape, (tuple, list))
    return pl.pallas_call(
        body,
        out_shape=out_shape,
        in_specs=whole(len(inputs)),
        out_specs=whole(len(out_shape)) if several else whole(1)[0],
        scratch_shapes=scratch,
        compiler_params=pltpu.CompilerParams(vmem_limit_bytes=limit),
    )(*inputs)


def iota(shape, axis):
    return lax.broadcasted_iota(jnp.int32, shape, axis)


def fold(rows):
    sub = iota((SUB, NB), 0)
    step = 1
    while len(rows) > 1:
        keep = (sub & step) == 0
        rows = [
            jnp.where(keep, a, b) + pltpu.roll(jnp.where(keep, b, a), step, 0)
            for a, b in zip(rows[0::2], rows[1::2])
        ]
        step *= 2
    return rows[0]


def take_lanes(value, index):
    return jnp.take_along_axis(value, index, axis=1, mode="promise_in_bounds")


def pick(fields, links_ref):
    odd = lax.axis_index("plan") & 1
    numbers = (0, 4 - odd, 3 + odd, 2, 1)
    picked = []
    for which in range(3):
        link = jnp.broadcast_to(links_ref[which], (BS, NB))
        lane, part = link & (NB - 1), link >> 7
        value = take_lanes(fields[0], lane)
        for number, field in zip(numbers[1:], fields[1:]):
            value = jnp.where(part == number, take_lanes(field, lane), value)
        picked.append(value)
    return picked


def coupled(weights_ref, picked, tile):
    rows = []
    for row in range(SUB):
        total = None
        for which in range(3):
            product = weights_ref[which, tile * SUB + row].astype(F32) * picked[which]
            for part in range(GROUPS):
                piece = product[part * SUB : (part + 1) * SUB]
                total = piece if total is None else total + piece
        rows.append(total)
    return fold(rows)


def tiles(step):
    def body(tile, carry):
        step(tile, pl.ds(pl.multiple_of(tile * SUB, SUB), SUB))
        return carry

    lax.fori_loop(0, GROUPS, body, 0)


def first_body(source, inner, outer, above, below, weights, links, owners, second):
    fields = [ref[...] for ref in (source, inner, outer, above, below)]
    picked = pick(fields, links)

    def step(tile, rows):
        mine = source[rows, :]
        applied = 0.5 * (mine + coupled(weights, picked, tile))
        second[rows, :] = 0.5 * mine + 0.5 * (mine - applied)

    tiles(step)
    second[BS:, :] = jnp.broadcast_to(owners[...].astype(F32), (SUB, NB))


def second_body(field, inner, outer, above, below, weights, links, source, owners, sent, left):
    fields = [ref[0:BS, :] for ref in (field, inner, outer, above, below)]
    picked = pick(fields, links)

    def step(tile, rows):
        left[rows, :] = source[rows, :] - (field[rows, :] + coupled(weights, picked, tile))

    tiles(step)
    member = ((iota((NB, NB), 0) & (NC - 1)) == owners[...]).astype(F32)
    spread = lax.dot_general(
        left[...],
        member,
        (((1,), (1,)), ((), ())),
        precision=lax.Precision.HIGHEST,
        preferred_element_type=F32,
    )
    lane_group = iota((SUB, NB), 1) // NC
    packed = spread[0:SUB]
    for group in range(1, GROUPS):
        packed = jnp.where(lane_group == group, spread[group * SUB : (group + 1) * SUB], packed)
    packed = packed * math.sqrt(NC / NB)
    for copy in range(sent.shape[0]):
        sent[copy] = packed


def last_body(field, inner, outer, above, below, errors, weights, links, source, out, third):
    fields = []
    for number, ref in enumerate((field, inner, outer, above, below)):
        error = errors[number]
        owner = ref[BS:, :].astype(jnp.int32)
        added = [take_lanes(error, owner + group * NC) for group in range(GROUPS)]
        fields.append(ref[0:BS, :] + jnp.concatenate(added, axis=0))
    third[...] = fields[0]
    picked = pick(fields, links)

    def step(tile, rows):
        mine = third[rows, :]
        applied = mine + coupled(weights, picked, tile)
        out[rows, :] = mine + 0.5 * (source[rows, :] - applied)

    tiles(step)


def skew(values, count):
    group = iota((SUB, NB), 1) // NC
    values = [v if g == 0 else pltpu.roll(v, NC * g, 1) for g, v in enumerate(values)]
    wanted = [(GROUPS - level) % GROUPS for level in range(count)]
    needed = [set(wanted)]
    for bit in (4, 2):
        needed.append({v for v in needed[-1]} | {(v + bit) % GROUPS for v in needed[-1]})
    for bit, places in zip((1, 2, 4), reversed(needed)):
        second = (group & bit) != 0
        values = [
            jnp.where(second, values[(v + bit) % GROUPS], values[v]) if v in places else None
            for v in range(GROUPS)
        ]
    return [values[v] for v in wanted]


def pack_body(source, packed, high):
    count = packed.shape[0]
    rest = (count - GROUPS) * NC

    def body(inner, carry):
        for part in range(GROUPS):
            high[part, :, 0:rest] = source[part, inner, :, NB:].astype(F32)
        for column in range(GROUPS):
            rows = slice(column * SUB, (column + 1) * SUB)
            place = column * SUB + inner
            values = [source[part, inner, rows, 0:NB].astype(F32) for part in range(GROUPS)]
            for level, value in enumerate(skew(values, GROUPS)):
                packed[level, place] = value
            values = [high[part, rows, :] for part in range(GROUPS)]
            for level, value in enumerate(skew(values, count - GROUPS)):
                packed[GROUPS + level, place] = value
        return carry

    lax.fori_loop(0, SUB, body, 0)


def pack(blocks):
    width = blocks.shape[2]
    return call(
        pack_body,
        jax.ShapeDtypeStruct((width // NC, BS, SUB, NB), F32),
        (blocks.reshape(GROUPS, SUB, BS, width),),
        12 * MIB,
        [pltpu.VMEM((GROUPS, BS, NB), F32)],
    )


def block_product(packed, level, vectors, turned):
    if len(vectors) > BATCH:
        parts = [vectors[i : i + BATCH] for i in range(0, len(vectors), BATCH)]
        return [out for part in parts for out in block_product(packed, level, part, turned)]
    lane = iota((SUB, NB), 1) & (NC - 1)
    totals = [[None] * SUB for _ in vectors]
    for column in range(GROUPS):
        place = lane + ((column + turned) % GROUPS) * NC
        spread = [take_lanes(v, place) for v in vectors]
        for row in range(SUB):
            weight = packed[level, column * SUB + row]
            for total, value in zip(totals, spread):
                piece = weight * value
                total[row] = piece if total[row] is None else total[row] + piece
    return [fold(total) for total in totals]


def up_step(ops, smooth, level, lows, highs):
    columns = lows + highs
    smoothed = block_product(smooth, level, columns, max(level - 1, 0))
    if level > 0:
        columns = [pltpu.roll(v, NC, 1) for v in columns]
    removed = block_product(ops, level, smoothed[len(lows) :], level)
    saved = list(zip(columns, smoothed[: len(lows)]))
    return saved, [a - b for a, b in zip(columns[len(lows) :], removed)]


def down_step(ops, smooth, level, errors, saved):
    totals = []
    for number, error in enumerate(errors):
        total = pltpu.roll(saved[number][1], NC, 1) if saved else error
        totals.append(total if error is None or not saved else total + error)
    applied = block_product(ops, level, totals, level + 1)
    if saved:
        applied = [a - g for a, (g, _) in zip(applied, saved)]
    fixed = block_product(smooth, level, applied, level)
    return [pltpu.roll(t, NB - NC, 1) - f for t, f in zip(totals, fixed)]


def group_sum(load, member, bits):
    start = (member >> bits) << bits
    total = load(start)
    for other in range(1, 2**bits):
        total = total + load(start + other)
    return total * 2.0 ** (-bits / 2)


def near_body(ops, smooth, received, sent, kept):
    count = received.shape[0]
    bits = count.bit_length() - 1
    me = lax.axis_index("plan") & (count - 1)
    across = (((me - 1) ^ 1) + 1) & (count - 1)
    load = lambda n: received[n]
    lows = [load(me), load(me ^ 1), load(across)]
    highs = []
    for level in range(1, bits):
        highs += [group_sum(load, me, level), group_sum(load, across, level)]
    highs.append(group_sum(load, me, bits))
    saved = []
    for level in range(bits):
        pairs, rest = up_step(ops, smooth, level, lows, highs)
        saved.append(pairs)
        lows, highs = rest[:2], rest[2:]
    errors = [None, None]
    for level in reversed(range(1, bits)):
        errors = down_step(ops, smooth, level, errors, saved[level])
    errors = down_step(ops, smooth, 0, [errors[0], errors[0], errors[1]], saved[0])
    for copy in range(sent.shape[0]):
        sent[copy, 0] = lows[0]
        sent[copy, 1] = errors[2]
    kept[0] = errors[0]
    kept[1] = errors[1]


def far_body(first, ops, smooth, received, near, sent, kept):
    count = received.shape[0]
    bits = count.bit_length() - 1
    members = 2**first
    place = lax.axis_index("plan")
    me, inside = place >> first, place & (members - 1)
    across = me - (inside == 0).astype(jnp.int32) + (inside == members - 1).astype(jnp.int32)
    across = jnp.clip(across, 0, count - 1)
    load = lambda n: received[n, 0]
    lows = [load(me), load(across)]
    highs = []
    for level in range(1, bits):
        highs += [group_sum(load, me, level), group_sum(load, across, level)]
    highs.append(group_sum(load, me, bits))
    saved = []
    for level in range(bits):
        pairs, rest = up_step(ops, smooth, first + level, lows, highs)
        saved.append(pairs)
        lows, highs = rest[:2], rest[2:]
    errors = [None, None]
    for level in reversed(range(bits)):
        errors = down_step(ops, smooth, first + level, errors, saved[level])
    for copy in range(sent.shape[0]):
        sent[copy, 0] = lows[0]
        sent[copy, 1] = near[0]
        sent[copy, 2] = errors[0]
    kept[0] = errors[1]
    kept[1] = received[across, 1]


def top_body(first, middle, ops, smooth, received, near, far, errors, tree):
    count = received.shape[0]
    bits = count.bit_length() - 1
    me, place = lax.axis_index("height"), lax.axis_index("plan")
    last = lax.axis_size("plan") - 1
    targets = (me, jnp.minimum(me + 1, count - 1), jnp.maximum(me - 1, 0))
    values = [received[n, 0] for n in range(count)]
    starts = []
    used = 0
    for level in range(first, LEVELS):
        pairs, _ = up_step(ops, smooth, level, values, [])
        removed = block_product(ops, level, [z for _, z in pairs], level)
        starts.append(used)
        for g, z in pairs:
            tree[used, 0] = g
            tree[used, 1] = z
            used += 1
        rest = [g - r for (g, _), r in zip(pairs, removed)]
        values = [(a + b) * HALF_ROOT for a, b in zip(rest[0::2], rest[1::2])]
    (error,) = block_product(smooth, LEVELS, values, LEVELS - 1)
    parts = [error] * len(targets)
    for level in reversed(range(first, LEVELS)):
        at = [starts[level - first] + (target >> (level - first)) for target in targets]
        saved = [(tree[n, 0], tree[n, 1]) for n in at]
        parts = down_step(ops, smooth, level, parts, saved)
    for level in reversed(range(middle, first)):
        parts = down_step(ops, smooth, level, parts, None)
    parts = [
        parts[0] + received[targets[0], 2],
        parts[0] + far[0],
        parts[1] + received[targets[1], 2],
        parts[2] + received[targets[2], 2],
    ]
    for level in reversed(range(middle)):
        parts = down_step(ops, smooth, level, parts, None)
    zero = jnp.zeros((SUB, NB), F32)
    errors[0] = parts[0] + near[0]
    errors[1] = parts[0] + near[1]
    errors[2] = jnp.where((place > 0) & (place < last), parts[1] + far[1], zero)
    errors[3] = jnp.where(me < count - 1, parts[2] + received[targets[1], 1], zero)
    errors[4] = jnp.where(me > 0, parts[3] + received[targets[2], 1], zero)


def shifted(value, step):
    count = lax.axis_size("height")
    pairs = [(i, i + step) for i in range(count) if 0 <= i + step < count]
    return lax.ppermute(value, "height", pairs)


def swapped(value, first):
    pairs = []
    for low in range(first, lax.axis_size("plan") - 1, 2):
        pairs += [(low, low + 1), (low + 1, low)]
    return lax.ppermute(value, "plan", pairs)


def halo(value):
    inner, outer = swapped(value, 0), swapped(value, 1)
    above, below = shifted(value, -1), shifted(value, 1)
    return inner, outer, above, below


def exchange(value, axis, groups=None):
    return lax.all_to_all(value, axis, 0, 0, axis_index_groups=groups, tiled=True)


def shards(right_side, couplings, neighbours, aggregates, coarse_ops, coarse_smooth):
    source = right_side[0, 0]
    weights = couplings[0, 0]
    links = neighbours[0, 0][:, None, :]
    owners = aggregates[0]
    plan = lax.axis_size("plan")
    height = lax.axis_size("height")
    plan_bits = plan.bit_length() - 1
    low_bits = (plan_bits + 1) // 2
    near = 2**low_bits
    far = plan // near
    field_shape = jax.ShapeDtypeStruct((BS, NB), F32)

    def vectors(*counts):
        return jax.ShapeDtypeStruct((*counts, SUB, NB), F32)

    smooth = pack(coarse_smooth)
    around = halo(source)
    smooth, source = lax.optimization_barrier((smooth, source))
    second = call(
        first_body,
        jax.ShapeDtypeStruct((BS + SUB, NB), F32),
        (source, *around, weights, links, owners),
        12 * MIB,
    )
    around = halo(second)
    second, coarse_ops = lax.optimization_barrier((second, coarse_ops))
    ops = pack(coarse_ops)
    ops, source = lax.optimization_barrier((ops, source))
    sent = call(
        second_body,
        vectors(near),
        (second, *around, weights, links, source, owners),
        12 * MIB,
        [pltpu.VMEM((BS, NB), F32)],
    )
    near_groups = [[a * near + b for b in range(near)] for a in range(far)]
    far_groups = [[a * near + b for a in range(far)] for b in range(near)]
    received = exchange(sent, "plan", near_groups)
    sent, near_kept = call(
        near_body, (vectors(far, 2), vectors(2)), (ops, smooth, received), 16 * MIB
    )
    received = exchange(sent, "plan", far_groups)
    sent, far_kept = call(
        functools.partial(far_body, low_bits),
        (vectors(height, 3), vectors(2)),
        (ops, smooth, received, near_kept),
        16 * MIB,
    )
    received = exchange(sent, "height")
    errors = call(
        functools.partial(top_body, plan_bits, low_bits),
        vectors(5),
        (ops, smooth, received, near_kept, far_kept),
        16 * MIB,
        [pltpu.VMEM((2 * height, 2, SUB, NB), F32)],
    )
    out = call(
        last_body,
        field_shape,
        (second, *around, errors, weights, links, source),
        12 * MIB,
        [pltpu.VMEM((BS, NB), F32)],
    )
    return out[None, None]


def solution(mesh):
    in_specs = (
        P("plan", "height", None, None),
        P("plan", "height", None, None, None, None),
        P("plan", "height", None, None),
        P("plan", "height", None),
        P(),
        P(),
    )
    out_specs = P("plan", "height", None, None)
    return jax.shard_map(shards, mesh=mesh, in_specs=in_specs, out_specs=out_specs, check_vma=False)
```

```python
import functools
import math

import jax
import jax.numpy as jnp
from jax import lax
from jax.experimental import pallas as pl
from jax.experimental.pallas import tpu as pltpu
from jax.sharding import PartitionSpec as P

BS = 64
NB = 128
NC = 16
LEVELS = 10
SUB = 8
GROUPS = BS // SUB
F32 = jnp.float32
MIB = 1 << 20
HALF_ROOT = 0.7071067811865476
BATCH = 4


def whole(count):
    return [pl.BlockSpec(memory_space=pltpu.VMEM)] * count


def call(body, out_shape, inputs, limit, scratch=()):
    several = isinstance(out_shape, (tuple, list))
    return pl.pallas_call(
        body,
        out_shape=out_shape,
        in_specs=whole(len(inputs)),
        out_specs=whole(len(out_shape)) if several else whole(1)[0],
        scratch_shapes=scratch,
        compiler_params=pltpu.CompilerParams(vmem_limit_bytes=limit),
    )(*inputs)


def iota(shape, axis):
    return lax.broadcasted_iota(jnp.int32, shape, axis)


def fold(rows):
    sub = iota((SUB, NB), 0)
    step = 1
    while len(rows) > 1:
        keep = (sub & step) == 0
        rows = [
            jnp.where(keep, a, b) + pltpu.roll(jnp.where(keep, b, a), step, 0)
            for a, b in zip(rows[0::2], rows[1::2])
        ]
        step *= 2
    return rows[0]


def take_lanes(value, index):
    return jnp.take_along_axis(value, index, axis=1, mode="promise_in_bounds")


def pick(fields, links_ref):
    odd = lax.axis_index("plan") & 1
    numbers = (0, 4 - odd, 3 + odd, 2, 1)
    picked = []
    for which in range(3):
        link = jnp.broadcast_to(links_ref[which], (BS, NB))
        lane, part = link & (NB - 1), link >> 7
        value = take_lanes(fields[0], lane)
        for number, field in zip(numbers[1:], fields[1:]):
            value = jnp.where(part == number, take_lanes(field, lane), value)
        picked.append(value)
    return picked


def coupled(weights_ref, picked, tile):
    rows = []
    for row in range(SUB):
        total = None
        for which in range(3):
            product = weights_ref[which, tile * SUB + row].astype(F32) * picked[which]
            for part in range(GROUPS):
                piece = product[part * SUB : (part + 1) * SUB]
                total = piece if total is None else total + piece
        rows.append(total)
    return fold(rows)


def tiles(step):
    def body(tile, carry):
        step(tile, pl.ds(pl.multiple_of(tile * SUB, SUB), SUB))
        return carry

    lax.fori_loop(0, GROUPS, body, 0)


def first_body(
    source, inner, outer, above, below, couplings, links, owners, blocks,
    second, weights, packed, field, link, owner, high, held, sems,
):
    small = [
        pltpu.make_async_copy(there, here, sems.at[2, number])
        for number, (there, here) in enumerate(((source, field), (links, link), (owners, owner)))
    ]

    def tile_copies(tile):
        rows = pl.ds(tile * SUB, SUB)
        return (
            pltpu.make_async_copy(couplings.at[:, rows], weights.at[:, rows], sems.at[0, tile]),
            pltpu.make_async_copy(blocks.at[:, tile], held.at[tile], sems.at[1, tile]),
        )

    for copy in small:
        copy.start()
    for tile in range(GROUPS):
        for copy in tile_copies(tile):
            copy.start()
    for copy in small:
        copy.wait()
    fields = [ref[...] for ref in (field, inner, outer, above, below)]
    picked = pick(fields, link)

    def step(tile, rows):
        for copy in tile_copies(tile):
            copy.wait()
        mine = field[rows, :]
        applied = 0.5 * (mine + coupled(weights, picked, tile))
        second[rows, :] = 0.5 * mine + 0.5 * (mine - applied)
        pack_rows(tile, lambda part, rows, lanes: held[tile, part, rows, lanes], high, packed)

    tiles(step)
    second[BS:, :] = jnp.broadcast_to(owner[...].astype(F32), (SUB, NB))


def second_body(field, inner, outer, above, below, weights, links, source, owners, blocks, sent, packed, left, high):
    fields = [ref[0:BS, :] for ref in (field, inner, outer, above, below)]
    picked = pick(fields, links)

    def step(tile, rows):
        left[rows, :] = source[rows, :] - (field[rows, :] + coupled(weights, picked, tile))
        pack_rows(tile, lambda part, rows, lanes: blocks[part, tile, rows, lanes], high, packed)

    tiles(step)
    member = ((iota((NB, NB), 0) & (NC - 1)) == owners[...]).astype(F32)
    spread = lax.dot_general(
        left[...],
        member,
        (((1,), (1,)), ((), ())),
        precision=lax.Precision.HIGHEST,
        preferred_element_type=F32,
    )
    lane_group = iota((SUB, NB), 1) // NC
    joined = spread[0:SUB]
    for group in range(1, GROUPS):
        joined = jnp.where(lane_group == group, spread[group * SUB : (group + 1) * SUB], joined)
    joined = joined * math.sqrt(NC / NB)
    for copy in range(sent.shape[0]):
        sent[copy] = joined


def last_body(field, inner, outer, above, below, errors, weights, links, source, out, third, stage, sems):
    fields = []
    for number, ref in enumerate((field, inner, outer, above, below)):
        error = errors[number]
        owner = ref[BS:, :].astype(jnp.int32)
        added = [take_lanes(error, owner + group * NC) for group in range(GROUPS)]
        fields.append(ref[0:BS, :] + jnp.concatenate(added, axis=0))
    third[...] = fields[0]
    picked = pick(fields, links)

    def step(tile, rows):
        mine = third[rows, :]
        applied = mine + coupled(weights, picked, tile)
        stage[rows, :] = mine + 0.5 * (source[rows, :] - applied)
        pltpu.make_async_copy(stage.at[rows], out.at[rows], sems.at[tile]).start()

    tiles(step)
    for tile in range(GROUPS):
        rows = pl.ds(tile * SUB, SUB)
        pltpu.make_async_copy(stage.at[rows], out.at[rows], sems.at[tile]).wait()


def skew(values, count):
    group = iota((SUB, NB), 1) // NC
    values = [v if g == 0 else pltpu.roll(v, NC * g, 1) for g, v in enumerate(values)]
    wanted = [(GROUPS - level) % GROUPS for level in range(count)]
    needed = [set(wanted)]
    for bit in (4, 2):
        needed.append({v for v in needed[-1]} | {(v + bit) % GROUPS for v in needed[-1]})
    for bit, places in zip((1, 2, 4), reversed(needed)):
        second = (group & bit) != 0
        values = [
            jnp.where(second, values[(v + bit) % GROUPS], values[v]) if v in places else None
            for v in range(GROUPS)
        ]
    return [values[v] for v in wanted]


def pack_rows(inner, load, high, packed):
    count = packed.shape[0]
    for part in range(GROUPS):
        high[part, :, 0 : (count - GROUPS) * NC] = load(part, slice(None), slice(NB, None)).astype(F32)
    for column in range(GROUPS):
        rows = slice(column * SUB, (column + 1) * SUB)
        place = column * SUB + inner
        values = [load(part, rows, slice(0, NB)).astype(F32) for part in range(GROUPS)]
        for level, value in enumerate(skew(values, GROUPS)):
            packed[level, place] = value
        values = [high[part, rows, :] for part in range(GROUPS)]
        for level, value in enumerate(skew(values, count - GROUPS)):
            packed[GROUPS + level, place] = value


def block_product(packed, level, vectors, turned):
    if len(vectors) > BATCH:
        parts = [vectors[i : i + BATCH] for i in range(0, len(vectors), BATCH)]
        return [out for part in parts for out in block_product(packed, level, part, turned)]
    lane = iota((SUB, NB), 1) & (NC - 1)
    totals = [[None] * SUB for _ in vectors]
    for column in range(GROUPS):
        place = lane + ((column + turned) % GROUPS) * NC
        spread = [take_lanes(v, place) for v in vectors]
        for row in range(SUB):
            weight = packed[level, column * SUB + row]
            for total, value in zip(totals, spread):
                piece = weight * value
                total[row] = piece if total[row] is None else total[row] + piece
    return [fold(total) for total in totals]


def up_step(ops, smooth, level, lows, highs):
    columns = lows + highs
    smoothed = block_product(smooth, level, columns, max(level - 1, 0))
    if level > 0:
        columns = [pltpu.roll(v, NC, 1) for v in columns]
    removed = block_product(ops, level, smoothed[len(lows) :], level)
    saved = list(zip(columns, smoothed[: len(lows)]))
    return saved, [a - b for a, b in zip(columns[len(lows) :], removed)]


def down_step(ops, smooth, level, errors, saved):
    totals = []
    for number, error in enumerate(errors):
        total = pltpu.roll(saved[number][1], NC, 1) if saved else error
        totals.append(total if error is None or not saved else total + error)
    applied = block_product(ops, level, totals, level + 1)
    if saved:
        applied = [a - g for a, (g, _) in zip(applied, saved)]
    fixed = block_product(smooth, level, applied, level)
    return [pltpu.roll(t, NB - NC, 1) - f for t, f in zip(totals, fixed)]


def group_sum(load, member, bits):
    start = (member >> bits) << bits
    total = load(start)
    for other in range(1, 2**bits):
        total = total + load(start + other)
    return total * 2.0 ** (-bits / 2)


def near_body(ops, smooth, received, sent, kept):
    count = received.shape[0]
    bits = count.bit_length() - 1
    me = lax.axis_index("plan") & (count - 1)
    across = (((me - 1) ^ 1) + 1) & (count - 1)
    load = lambda n: received[n]
    lows = [load(me), load(me ^ 1), load(across)]
    highs = []
    for level in range(1, bits):
        highs += [group_sum(load, me, level), group_sum(load, across, level)]
    highs.append(group_sum(load, me, bits))
    saved = []
    for level in range(bits):
        pairs, rest = up_step(ops, smooth, level, lows, highs)
        saved.append(pairs)
        lows, highs = rest[:2], rest[2:]
    errors = [None, None]
    for level in reversed(range(1, bits)):
        errors = down_step(ops, smooth, level, errors, saved[level])
    errors = down_step(ops, smooth, 0, [errors[0], errors[0], errors[1]], saved[0])
    for copy in range(sent.shape[0]):
        sent[copy, 0] = lows[0]
        sent[copy, 1] = errors[2]
    kept[0] = errors[0]
    kept[1] = errors[1]


def far_body(first, ops, smooth, received, near, sent, kept):
    count = received.shape[0]
    bits = count.bit_length() - 1
    members = 2**first
    place = lax.axis_index("plan")
    me, inside = place >> first, place & (members - 1)
    across = me - (inside == 0).astype(jnp.int32) + (inside == members - 1).astype(jnp.int32)
    across = jnp.clip(across, 0, count - 1)
    load = lambda n: received[n, 0]
    lows = [load(me), load(across)]
    highs = []
    for level in range(1, bits):
        highs += [group_sum(load, me, level), group_sum(load, across, level)]
    highs.append(group_sum(load, me, bits))
    saved = []
    for level in range(bits):
        pairs, rest = up_step(ops, smooth, first + level, lows, highs)
        saved.append(pairs)
        lows, highs = rest[:2], rest[2:]
    errors = [None, None]
    for level in reversed(range(bits)):
        errors = down_step(ops, smooth, first + level, errors, saved[level])
    for copy in range(sent.shape[0]):
        sent[copy, 0] = lows[0]
        sent[copy, 1] = near[0]
        sent[copy, 2] = errors[0]
    kept[0] = errors[1]
    kept[1] = received[across, 1]


def top_body(first, middle, ops, smooth, received, near, far, errors, tree):
    count = received.shape[0]
    bits = count.bit_length() - 1
    me, place = lax.axis_index("height"), lax.axis_index("plan")
    last = lax.axis_size("plan") - 1
    targets = (me, jnp.minimum(me + 1, count - 1), jnp.maximum(me - 1, 0))
    values = [received[n, 0] for n in range(count)]
    starts = []
    used = 0
    for level in range(first, LEVELS):
        pairs, _ = up_step(ops, smooth, level, values, [])
        removed = block_product(ops, level, [z for _, z in pairs], level)
        starts.append(used)
        for g, z in pairs:
            tree[used, 0] = g
            tree[used, 1] = z
            used += 1
        rest = [g - r for (g, _), r in zip(pairs, removed)]
        values = [(a + b) * HALF_ROOT for a, b in zip(rest[0::2], rest[1::2])]
    (error,) = block_product(smooth, LEVELS, values, LEVELS - 1)
    parts = [error] * len(targets)
    for level in reversed(range(first, LEVELS)):
        at = [starts[level - first] + (target >> (level - first)) for target in targets]
        saved = [(tree[n, 0], tree[n, 1]) for n in at]
        parts = down_step(ops, smooth, level, parts, saved)
    for level in reversed(range(middle, first)):
        parts = down_step(ops, smooth, level, parts, None)
    parts = [
        parts[0] + received[targets[0], 2],
        parts[0] + far[0],
        parts[1] + received[targets[1], 2],
        parts[2] + received[targets[2], 2],
    ]
    for level in reversed(range(middle)):
        parts = down_step(ops, smooth, level, parts, None)
    zero = jnp.zeros((SUB, NB), F32)
    errors[0] = parts[0] + near[0]
    errors[1] = parts[0] + near[1]
    errors[2] = jnp.where((place > 0) & (place < last), parts[1] + far[1], zero)
    errors[3] = jnp.where(me < count - 1, parts[2] + received[targets[1], 1], zero)
    errors[4] = jnp.where(me > 0, parts[3] + received[targets[2], 1], zero)


def shifted(value, step):
    count = lax.axis_size("height")
    pairs = [(i, i + step) for i in range(count) if 0 <= i + step < count]
    return lax.ppermute(value, "height", pairs)


def swapped(value, first):
    pairs = []
    for low in range(first, lax.axis_size("plan") - 1, 2):
        pairs += [(low, low + 1), (low + 1, low)]
    return lax.ppermute(value, "plan", pairs)


def halo(value):
    inner, outer = swapped(value, 0), swapped(value, 1)
    above, below = shifted(value, -1), shifted(value, 1)
    return inner, outer, above, below


def exchange(value, axis, groups=None):
    return lax.all_to_all(value, axis, 0, 0, axis_index_groups=groups, tiled=True)


def shards(right_side, couplings, neighbours, aggregates, coarse_ops, coarse_smooth):
    source = right_side[0, 0]
    weights = couplings[0, 0]
    links = neighbours[0, 0][:, None, :]
    owners = aggregates[0]
    plan = lax.axis_size("plan")
    height = lax.axis_size("height")
    plan_bits = plan.bit_length() - 1
    low_bits = (plan_bits + 1) // 2
    near = 2**low_bits
    far = plan // near
    field_shape = jax.ShapeDtypeStruct((BS, NB), F32)

    def vectors(*counts):
        return jax.ShapeDtypeStruct((*counts, SUB, NB), F32)

    weights_type = jax.ShapeDtypeStruct(weights.shape, weights.dtype)
    split = lambda blocks: blocks.reshape(GROUPS, SUB, BS, blocks.shape[2])
    high = pltpu.VMEM((GROUPS, BS, NB), F32)
    vmem, hbm = (pl.BlockSpec(memory_space=space) for space in (pltpu.VMEM, pltpu.HBM))
    held = functools.partial(pltpu.with_memory_space_constraint, memory_space=pltpu.HBM)
    second, weights, smooth = pl.pallas_call(
        first_body,
        out_shape=(
            jax.ShapeDtypeStruct((BS + SUB, NB), F32),
            weights_type,
            vectors(LEVELS + 1, BS),
        ),
        in_specs=[hbm] + [vmem] * 4 + [hbm] * 4,
        out_specs=(vmem, vmem, vmem),
        scratch_shapes=[
            pltpu.VMEM((BS, NB), F32),
            pltpu.VMEM(links.shape, links.dtype),
            pltpu.VMEM(owners.shape, owners.dtype),
            high,
            pltpu.VMEM((SUB, GROUPS, BS, coarse_smooth.shape[2]), coarse_smooth.dtype),
            pltpu.SemaphoreType.DMA((3, GROUPS)),
        ],
        compiler_params=pltpu.CompilerParams(vmem_limit_bytes=24 * MIB),
    )(
        held(source),
        *halo(source),
        held(weights),
        held(links),
        held(owners),
        held(split(coarse_smooth)),
    )
    around = halo(second)
    sent, ops = call(
        second_body,
        (vectors(near), vectors(LEVELS, BS)),
        (second, *around, weights, links, source, owners, split(coarse_ops)),
        24 * MIB,
        [pltpu.VMEM((BS, NB), F32), high],
    )
    near_groups = [[a * near + b for b in range(near)] for a in range(far)]
    far_groups = [[a * near + b for a in range(far)] for b in range(near)]
    received = exchange(sent, "plan", near_groups)
    sent, near_kept = call(
        near_body, (vectors(far, 2), vectors(2)), (ops, smooth, received), 16 * MIB
    )
    received = exchange(sent, "plan", far_groups)
    sent, far_kept = call(
        functools.partial(far_body, low_bits),
        (vectors(height, 3), vectors(2)),
        (ops, smooth, received, near_kept),
        16 * MIB,
    )
    received = exchange(sent, "height")
    errors = call(
        functools.partial(top_body, plan_bits, low_bits),
        vectors(5),
        (ops, smooth, received, near_kept, far_kept),
        16 * MIB,
        [pltpu.VMEM((2 * height, 2, SUB, NB), F32)],
    )
    out = pl.pallas_call(
        last_body,
        out_shape=field_shape,
        in_specs=[vmem] * 9,
        out_specs=hbm,
        scratch_shapes=[
            pltpu.VMEM((BS, NB), F32),
            pltpu.VMEM((BS, NB), F32),
            pltpu.SemaphoreType.DMA((GROUPS,)),
        ],
        compiler_params=pltpu.CompilerParams(vmem_limit_bytes=12 * MIB),
    )(second, *around, errors, weights, links, source)
    return out[None, None]


def solution(mesh):
    in_specs = (
        P("plan", "height", None, None),
        P("plan", "height", None, None, None, None),
        P("plan", "height", None, None),
        P("plan", "height", None),
        P(),
        P(),
    )
    out_specs = P("plan", "height", None, None)
    return jax.shard_map(shards, mesh=mesh, in_specs=in_specs, out_specs=out_specs, check_vma=False)
```

```python
import functools
import math

import jax
import jax.numpy as jnp
from jax import lax
from jax.experimental import pallas as pl
from jax.experimental.pallas import tpu as pltpu
from jax.sharding import PartitionSpec as P

BS = 64
NB = 128
NC = 16
LEVELS = 10
SUB = 8
GROUPS = BS // SUB
F32 = jnp.float32
MIB = 1 << 20
HALF_ROOT = 0.7071067811865476
BATCH = 4


def whole(count):
    return [pl.BlockSpec(memory_space=pltpu.VMEM)] * count


def call(body, out_shape, inputs, limit, scratch=()):
    several = isinstance(out_shape, (tuple, list))
    return pl.pallas_call(
        body,
        out_shape=out_shape,
        in_specs=whole(len(inputs)),
        out_specs=whole(len(out_shape)) if several else whole(1)[0],
        scratch_shapes=scratch,
        compiler_params=pltpu.CompilerParams(vmem_limit_bytes=limit),
    )(*inputs)


def iota(shape, axis):
    return lax.broadcasted_iota(jnp.int32, shape, axis)


def fold(rows):
    sub = iota((SUB, NB), 0)
    step = 1
    while len(rows) > 1:
        keep = (sub & step) == 0
        rows = [
            jnp.where(keep, a, b) + pltpu.roll(jnp.where(keep, b, a), step, 0)
            for a, b in zip(rows[0::2], rows[1::2])
        ]
        step *= 2
    return rows[0]


def take_lanes(value, index):
    return jnp.take_along_axis(value, index, axis=1, mode="promise_in_bounds")


def pick(fields, links_ref):
    odd = lax.axis_index("plan") & 1
    numbers = (0, 4 - odd, 3 + odd, 2, 1)
    picked = []
    for which in range(3):
        link = jnp.broadcast_to(links_ref[which], (BS, NB))
        lane, part = link & (NB - 1), link >> 7
        value = take_lanes(fields[0], lane)
        for number, field in zip(numbers[1:], fields[1:]):
            value = jnp.where(part == number, take_lanes(field, lane), value)
        picked.append(value)
    return picked


def coupled(weights_ref, picked, tile):
    rows = []
    for row in range(SUB):
        total = None
        for which in range(3):
            product = weights_ref[which, tile * SUB + row].astype(F32) * picked[which]
            for part in range(GROUPS):
                piece = product[part * SUB : (part + 1) * SUB]
                total = piece if total is None else total + piece
        rows.append(total)
    return fold(rows)


def tiles(step):
    def body(tile, carry):
        step(tile, pl.ds(pl.multiple_of(tile * SUB, SUB), SUB))
        return carry

    lax.fori_loop(0, GROUPS, body, 0)


def first_body(source, inner, outer, above, below, weights, links, owners, second):
    fields = [ref[...] for ref in (source, inner, outer, above, below)]
    picked = pick(fields, links)

    def step(tile, rows):
        mine = source[rows, :]
        applied = 0.5 * (mine + coupled(weights, picked, tile))
        second[rows, :] = 0.5 * mine + 0.5 * (mine - applied)

    tiles(step)
    second[BS:, :] = jnp.broadcast_to(owners[...].astype(F32), (SUB, NB))


def second_body(field, inner, outer, above, below, weights, links, source, owners, sent, left):
    fields = [ref[0:BS, :] for ref in (field, inner, outer, above, below)]
    picked = pick(fields, links)

    def step(tile, rows):
        left[rows, :] = source[rows, :] - (field[rows, :] + coupled(weights, picked, tile))

    tiles(step)
    member = ((iota((NB, NB), 0) & (NC - 1)) == owners[...]).astype(F32)
    spread = lax.dot_general(
        left[...],
        member,
        (((1,), (1,)), ((), ())),
        precision=lax.Precision.HIGHEST,
        preferred_element_type=F32,
    )
    lane_group = iota((SUB, NB), 1) // NC
    packed = spread[0:SUB]
    for group in range(1, GROUPS):
        packed = jnp.where(lane_group == group, spread[group * SUB : (group + 1) * SUB], packed)
    packed = packed * math.sqrt(NC / NB)
    for copy in range(sent.shape[0]):
        sent[copy] = packed


def last_body(field, inner, outer, above, below, errors, weights, links, source, out, third):
    fields = []
    for number, ref in enumerate((field, inner, outer, above, below)):
        error = errors[number]
        owner = ref[BS:, :].astype(jnp.int32)
        added = [take_lanes(error, owner + group * NC) for group in range(GROUPS)]
        fields.append(ref[0:BS, :] + jnp.concatenate(added, axis=0))
    third[...] = fields[0]
    picked = pick(fields, links)

    def step(tile, rows):
        mine = third[rows, :]
        applied = mine + coupled(weights, picked, tile)
        out[rows, :] = mine + 0.5 * (source[rows, :] - applied)

    tiles(step)


def skew(values, count):
    group = iota((SUB, NB), 1) // NC
    values = [v if g == 0 else pltpu.roll(v, NC * g, 1) for g, v in enumerate(values)]
    wanted = [(GROUPS - level) % GROUPS for level in range(count)]
    needed = [set(wanted)]
    for bit in (4, 2):
        needed.append({v for v in needed[-1]} | {(v + bit) % GROUPS for v in needed[-1]})
    for bit, places in zip((1, 2, 4), reversed(needed)):
        second = (group & bit) != 0
        values = [
            jnp.where(second, values[(v + bit) % GROUPS], values[v]) if v in places else None
            for v in range(GROUPS)
        ]
    return [values[v] for v in wanted]


def pack_rows(inner, load, high, packed):
    count = packed.shape[0]
    for part in range(GROUPS):
        high[part, :, 0 : (count - GROUPS) * NC] = load(part, slice(None), slice(NB, None)).astype(F32)
    for column in range(GROUPS):
        rows = slice(column * SUB, (column + 1) * SUB)
        place = column * SUB + inner
        values = [load(part, rows, slice(0, NB)).astype(F32) for part in range(GROUPS)]
        for level, value in enumerate(skew(values, GROUPS)):
            packed[level, place] = value
        values = [high[part, rows, :] for part in range(GROUPS)]
        for level, value in enumerate(skew(values, count - GROUPS)):
            packed[GROUPS + level, place] = value


def pack_body(source, packed, high):
    def body(inner, carry):
        pack_rows(inner, lambda part, rows, lanes: source[part, inner, rows, lanes], high, packed)
        return carry

    lax.fori_loop(0, SUB, body, 0)


def stream_body(source, packed, high, held, sems):
    def copy(inner):
        return pltpu.make_async_copy(source.at[:, inner], held.at[inner], sems.at[inner])

    for inner in range(SUB):
        copy(inner).start()

    def body(inner, carry):
        copy(inner).wait()
        pack_rows(inner, lambda part, rows, lanes: held[inner, part, rows, lanes], high, packed)
        return carry

    lax.fori_loop(0, SUB, body, 0)


def pack(blocks, streamed):
    width = blocks.shape[2]
    blocks = blocks.reshape(GROUPS, SUB, BS, width)
    scratch = [pltpu.VMEM((GROUPS, BS, NB), F32)]
    if streamed:
        blocks = pltpu.with_memory_space_constraint(blocks, pltpu.HBM)
        scratch += [
            pltpu.VMEM((SUB, GROUPS, BS, width), blocks.dtype),
            pltpu.SemaphoreType.DMA((SUB,)),
        ]
    return pl.pallas_call(
        stream_body if streamed else pack_body,
        out_shape=jax.ShapeDtypeStruct((width // NC, BS, SUB, NB), F32),
        in_specs=[pl.BlockSpec(memory_space=pltpu.HBM if streamed else pltpu.VMEM)],
        out_specs=pl.BlockSpec(memory_space=pltpu.VMEM),
        scratch_shapes=scratch,
        compiler_params=pltpu.CompilerParams(vmem_limit_bytes=12 * MIB),
    )(blocks)


def block_product(packed, level, vectors, turned):
    if len(vectors) > BATCH:
        parts = [vectors[i : i + BATCH] for i in range(0, len(vectors), BATCH)]
        return [out for part in parts for out in block_product(packed, level, part, turned)]
    lane = iota((SUB, NB), 1) & (NC - 1)
    totals = [[None] * SUB for _ in vectors]
    for column in range(GROUPS):
        place = lane + ((column + turned) % GROUPS) * NC
        spread = [take_lanes(v, place) for v in vectors]
        for row in range(SUB):
            weight = packed[level, column * SUB + row]
            for total, value in zip(totals, spread):
                piece = weight * value
                total[row] = piece if total[row] is None else total[row] + piece
    return [fold(total) for total in totals]


def up_step(ops, smooth, level, lows, highs):
    columns = lows + highs
    smoothed = block_product(smooth, level, columns, max(level - 1, 0))
    if level > 0:
        columns = [pltpu.roll(v, NC, 1) for v in columns]
    removed = block_product(ops, level, smoothed[len(lows) :], level)
    saved = list(zip(columns, smoothed[: len(lows)]))
    return saved, [a - b for a, b in zip(columns[len(lows) :], removed)]


def down_step(ops, smooth, level, errors, saved):
    totals = []
    for number, error in enumerate(errors):
        total = pltpu.roll(saved[number][1], NC, 1) if saved else error
        totals.append(total if error is None or not saved else total + error)
    applied = block_product(ops, level, totals, level + 1)
    if saved:
        applied = [a - g for a, (g, _) in zip(applied, saved)]
    fixed = block_product(smooth, level, applied, level)
    return [pltpu.roll(t, NB - NC, 1) - f for t, f in zip(totals, fixed)]


def group_sum(load, member, bits):
    start = (member >> bits) << bits
    total = load(start)
    for other in range(1, 2**bits):
        total = total + load(start + other)
    return total * 2.0 ** (-bits / 2)


def near_body(ops, smooth, received, sent, kept):
    count = received.shape[0]
    bits = count.bit_length() - 1
    me = lax.axis_index("plan") & (count - 1)
    across = (((me - 1) ^ 1) + 1) & (count - 1)
    load = lambda n: received[n]
    lows = [load(me), load(me ^ 1), load(across)]
    highs = []
    for level in range(1, bits):
        highs += [group_sum(load, me, level), group_sum(load, across, level)]
    highs.append(group_sum(load, me, bits))
    saved = []
    for level in range(bits):
        pairs, rest = up_step(ops, smooth, level, lows, highs)
        saved.append(pairs)
        lows, highs = rest[:2], rest[2:]
    errors = [None, None]
    for level in reversed(range(1, bits)):
        errors = down_step(ops, smooth, level, errors, saved[level])
    errors = down_step(ops, smooth, 0, [errors[0], errors[0], errors[1]], saved[0])
    for copy in range(sent.shape[0]):
        sent[copy, 0] = lows[0]
        sent[copy, 1] = errors[2]
    kept[0] = errors[0]
    kept[1] = errors[1]


def far_body(first, ops, smooth, received, near, sent, kept):
    count = received.shape[0]
    bits = count.bit_length() - 1
    members = 2**first
    place = lax.axis_index("plan")
    me, inside = place >> first, place & (members - 1)
    across = me - (inside == 0).astype(jnp.int32) + (inside == members - 1).astype(jnp.int32)
    across = jnp.clip(across, 0, count - 1)
    load = lambda n: received[n, 0]
    lows = [load(me), load(across)]
    highs = []
    for level in range(1, bits):
        highs += [group_sum(load, me, level), group_sum(load, across, level)]
    highs.append(group_sum(load, me, bits))
    saved = []
    for level in range(bits):
        pairs, rest = up_step(ops, smooth, first + level, lows, highs)
        saved.append(pairs)
        lows, highs = rest[:2], rest[2:]
    errors = [None, None]
    for level in reversed(range(bits)):
        errors = down_step(ops, smooth, first + level, errors, saved[level])
    for copy in range(sent.shape[0]):
        sent[copy, 0] = lows[0]
        sent[copy, 1] = near[0]
        sent[copy, 2] = errors[0]
    kept[0] = errors[1]
    kept[1] = received[across, 1]


def top_body(first, middle, ops, smooth, received, near, far, errors, tree):
    count = received.shape[0]
    bits = count.bit_length() - 1
    me, place = lax.axis_index("height"), lax.axis_index("plan")
    last = lax.axis_size("plan") - 1
    targets = (me, jnp.minimum(me + 1, count - 1), jnp.maximum(me - 1, 0))
    values = [received[n, 0] for n in range(count)]
    starts = []
    used = 0
    for level in range(first, LEVELS):
        pairs, _ = up_step(ops, smooth, level, values, [])
        removed = block_product(ops, level, [z for _, z in pairs], level)
        starts.append(used)
        for g, z in pairs:
            tree[used, 0] = g
            tree[used, 1] = z
            used += 1
        rest = [g - r for (g, _), r in zip(pairs, removed)]
        values = [(a + b) * HALF_ROOT for a, b in zip(rest[0::2], rest[1::2])]
    (error,) = block_product(smooth, LEVELS, values, LEVELS - 1)
    parts = [error] * len(targets)
    for level in reversed(range(first, LEVELS)):
        at = [starts[level - first] + (target >> (level - first)) for target in targets]
        saved = [(tree[n, 0], tree[n, 1]) for n in at]
        parts = down_step(ops, smooth, level, parts, saved)
    for level in reversed(range(middle, first)):
        parts = down_step(ops, smooth, level, parts, None)
    parts = [
        parts[0] + received[targets[0], 2],
        parts[0] + far[0],
        parts[1] + received[targets[1], 2],
        parts[2] + received[targets[2], 2],
    ]
    for level in reversed(range(middle)):
        parts = down_step(ops, smooth, level, parts, None)
    zero = jnp.zeros((SUB, NB), F32)
    errors[0] = parts[0] + near[0]
    errors[1] = parts[0] + near[1]
    errors[2] = jnp.where((place > 0) & (place < last), parts[1] + far[1], zero)
    errors[3] = jnp.where(me < count - 1, parts[2] + received[targets[1], 1], zero)
    errors[4] = jnp.where(me > 0, parts[3] + received[targets[2], 1], zero)


def shifted(value, step):
    count = lax.axis_size("height")
    pairs = [(i, i + step) for i in range(count) if 0 <= i + step < count]
    return lax.ppermute(value, "height", pairs)


def swapped(value, first):
    pairs = []
    for low in range(first, lax.axis_size("plan") - 1, 2):
        pairs += [(low, low + 1), (low + 1, low)]
    return lax.ppermute(value, "plan", pairs)


def halo(value):
    inner, outer = swapped(value, 0), swapped(value, 1)
    above, below = shifted(value, -1), shifted(value, 1)
    return inner, outer, above, below


def exchange(value, axis, groups=None):
    return lax.all_to_all(value, axis, 0, 0, axis_index_groups=groups, tiled=True)


def shards(right_side, couplings, neighbours, aggregates, coarse_ops, coarse_smooth):
    source = right_side[0, 0]
    weights = couplings[0, 0]
    links = neighbours[0, 0][:, None, :]
    owners = aggregates[0]
    plan = lax.axis_size("plan")
    height = lax.axis_size("height")
    plan_bits = plan.bit_length() - 1
    low_bits = (plan_bits + 1) // 2
    near = 2**low_bits
    far = plan // near
    field_shape = jax.ShapeDtypeStruct((BS, NB), F32)

    def vectors(*counts):
        return jax.ShapeDtypeStruct((*counts, SUB, NB), F32)

    smooth = pack(coarse_smooth, True)
    around = halo(source)
    smooth, source = lax.optimization_barrier((smooth, source))
    second = call(
        first_body,
        jax.ShapeDtypeStruct((BS + SUB, NB), F32),
        (source, *around, weights, links, owners),
        12 * MIB,
    )
    around = halo(second)
    second, coarse_ops = lax.optimization_barrier((second, coarse_ops))
    ops = pack(coarse_ops, False)
    ops, source = lax.optimization_barrier((ops, source))
    sent = call(
        second_body,
        vectors(near),
        (second, *around, weights, links, source, owners),
        12 * MIB,
        [pltpu.VMEM((BS, NB), F32)],
    )
    near_groups = [[a * near + b for b in range(near)] for a in range(far)]
    far_groups = [[a * near + b for a in range(far)] for b in range(near)]
    received = exchange(sent, "plan", near_groups)
    sent, near_kept = call(
        near_body, (vectors(far, 2), vectors(2)), (ops, smooth, received), 16 * MIB
    )
    received = exchange(sent, "plan", far_groups)
    sent, far_kept = call(
        functools.partial(far_body, low_bits),
        (vectors(height, 3), vectors(2)),
        (ops, smooth, received, near_kept),
        16 * MIB,
    )
    received = exchange(sent, "height")
    errors = call(
        functools.partial(top_body, plan_bits, low_bits),
        vectors(5),
        (ops, smooth, received, near_kept, far_kept),
        16 * MIB,
        [pltpu.VMEM((2 * height, 2, SUB, NB), F32)],
    )
    out = call(
        last_body,
        field_shape,
        (second, *around, errors, weights, links, source),
        12 * MIB,
        [pltpu.VMEM((BS, NB), F32)],
    )
    return out[None, None]


def solution(mesh):
    in_specs = (
        P("plan", "height", None, None),
        P("plan", "height", None, None, None, None),
        P("plan", "height", None, None),
        P("plan", "height", None),
        P(),
        P(),
    )
    out_specs = P("plan", "height", None, None)
    return jax.shard_map(shards, mesh=mesh, in_specs=in_specs, out_specs=out_specs, check_vma=False)
```

```python
import functools
import math

import jax
import jax.numpy as jnp
from jax import lax
from jax.experimental import pallas as pl
from jax.experimental.pallas import tpu as pltpu
from jax.sharding import PartitionSpec as P

BS = 64
NB = 128
NC = 16
LEVELS = 10
SUB = 8
GROUPS = BS // SUB
F32 = jnp.float32
MIB = 1 << 20
HALF_ROOT = 0.7071067811865476
BATCH = 4


def whole(count):
    return [pl.BlockSpec(memory_space=pltpu.VMEM)] * count


def call(body, out_shape, inputs, limit, scratch=()):
    several = isinstance(out_shape, (tuple, list))
    return pl.pallas_call(
        body,
        out_shape=out_shape,
        in_specs=whole(len(inputs)),
        out_specs=whole(len(out_shape)) if several else whole(1)[0],
        scratch_shapes=scratch,
        compiler_params=pltpu.CompilerParams(vmem_limit_bytes=limit),
    )(*inputs)


def iota(shape, axis):
    return lax.broadcasted_iota(jnp.int32, shape, axis)


def fold(rows):
    sub = iota((SUB, NB), 0)
    step = 1
    while len(rows) > 1:
        keep = (sub & step) == 0
        rows = [
            jnp.where(keep, a, b) + pltpu.roll(jnp.where(keep, b, a), step, 0)
            for a, b in zip(rows[0::2], rows[1::2])
        ]
        step *= 2
    return rows[0]


def take_lanes(value, index):
    return jnp.take_along_axis(value, index, axis=1, mode="promise_in_bounds")


def pick(fields, links_ref):
    odd = lax.axis_index("plan") & 1
    numbers = (0, 4 - odd, 3 + odd, 2, 1)
    picked = []
    for which in range(3):
        link = jnp.broadcast_to(links_ref[which], (BS, NB))
        lane, part = link & (NB - 1), link >> 7
        value = take_lanes(fields[0], lane)
        for number, field in zip(numbers[1:], fields[1:]):
            value = jnp.where(part == number, take_lanes(field, lane), value)
        picked.append(value)
    return picked


def coupled(weights_ref, picked, tile):
    rows = []
    for row in range(SUB):
        total = None
        for which in range(3):
            product = weights_ref[which, tile * SUB + row].astype(F32) * picked[which]
            for part in range(GROUPS):
                piece = product[part * SUB : (part + 1) * SUB]
                total = piece if total is None else total + piece
        rows.append(total)
    return fold(rows)


def tiles(step):
    def body(tile, carry):
        step(tile, pl.ds(pl.multiple_of(tile * SUB, SUB), SUB))
        return carry

    lax.fori_loop(0, GROUPS, body, 0)


def first_body(source, inner, outer, above, below, weights, links, owners, second):
    fields = [ref[...] for ref in (source, inner, outer, above, below)]
    picked = pick(fields, links)

    def step(tile, rows):
        mine = source[rows, :]
        applied = 0.5 * (mine + coupled(weights, picked, tile))
        second[rows, :] = 0.5 * mine + 0.5 * (mine - applied)

    tiles(step)
    second[BS:, :] = jnp.broadcast_to(owners[...].astype(F32), (SUB, NB))


def second_body(field, inner, outer, above, below, weights, links, source, owners, sent, left):
    fields = [ref[0:BS, :] for ref in (field, inner, outer, above, below)]
    picked = pick(fields, links)

    def step(tile, rows):
        left[rows, :] = source[rows, :] - (field[rows, :] + coupled(weights, picked, tile))

    tiles(step)
    member = ((iota((NB, NB), 0) & (NC - 1)) == owners[...]).astype(F32)
    spread = lax.dot_general(
        left[...],
        member,
        (((1,), (1,)), ((), ())),
        precision=lax.Precision.HIGHEST,
        preferred_element_type=F32,
    )
    lane_group = iota((SUB, NB), 1) // NC
    packed = spread[0:SUB]
    for group in range(1, GROUPS):
        packed = jnp.where(lane_group == group, spread[group * SUB : (group + 1) * SUB], packed)
    packed = packed * math.sqrt(NC / NB)
    for copy in range(sent.shape[0]):
        sent[copy] = packed


def last_body(field, inner, outer, above, below, errors, weights, links, source, out, third):
    fields = []
    for number, ref in enumerate((field, inner, outer, above, below)):
        error = errors[number]
        owner = ref[BS:, :].astype(jnp.int32)
        added = [take_lanes(error, owner + group * NC) for group in range(GROUPS)]
        fields.append(ref[0:BS, :] + jnp.concatenate(added, axis=0))
    third[...] = fields[0]
    picked = pick(fields, links)

    def step(tile, rows):
        mine = third[rows, :]
        applied = mine + coupled(weights, picked, tile)
        out[rows, :] = mine + 0.5 * (source[rows, :] - applied)

    tiles(step)


def skew(values, count):
    group = iota((SUB, NB), 1) // NC
    values = [v if g == 0 else pltpu.roll(v, NC * g, 1) for g, v in enumerate(values)]
    wanted = [(GROUPS - level) % GROUPS for level in range(count)]
    needed = [set(wanted)]
    for bit in (4, 2):
        needed.append({v for v in needed[-1]} | {(v + bit) % GROUPS for v in needed[-1]})
    for bit, places in zip((1, 2, 4), reversed(needed)):
        second = (group & bit) != 0
        values = [
            jnp.where(second, values[(v + bit) % GROUPS], values[v]) if v in places else None
            for v in range(GROUPS)
        ]
    return [values[v] for v in wanted]


def pack_rows(inner, load, high, packed):
    count = packed.shape[0]
    for part in range(GROUPS):
        high[part, :, 0 : (count - GROUPS) * NC] = load(part, slice(None), slice(NB, None)).astype(F32)
    for column in range(GROUPS):
        rows = slice(column * SUB, (column + 1) * SUB)
        place = column * SUB + inner
        values = [load(part, rows, slice(0, NB)).astype(F32) for part in range(GROUPS)]
        for level, value in enumerate(skew(values, GROUPS)):
            packed[level, place] = value
        values = [high[part, rows, :] for part in range(GROUPS)]
        for level, value in enumerate(skew(values, count - GROUPS)):
            packed[GROUPS + level, place] = value


def pack_body(source, packed, high):
    def body(inner, carry):
        pack_rows(inner, lambda part, rows, lanes: source[part, inner, rows, lanes], high, packed)
        return carry

    lax.fori_loop(0, SUB, body, 0)


def stream_body(source, packed, high, held, sems):
    def copy(inner):
        return pltpu.make_async_copy(source.at[:, inner], held.at[inner], sems.at[inner])

    for inner in range(SUB):
        copy(inner).start()

    def body(inner, carry):
        copy(inner).wait()
        pack_rows(inner, lambda part, rows, lanes: held[inner, part, rows, lanes], high, packed)
        return carry

    lax.fori_loop(0, SUB, body, 0)


def pack(blocks, streamed):
    width = blocks.shape[2]
    blocks = blocks.reshape(GROUPS, SUB, BS, width)
    scratch = [pltpu.VMEM((GROUPS, BS, NB), F32)]
    if streamed:
        blocks = pltpu.with_memory_space_constraint(blocks, pltpu.HBM)
        scratch += [
            pltpu.VMEM((SUB, GROUPS, BS, width), blocks.dtype),
            pltpu.SemaphoreType.DMA((SUB,)),
        ]
    return pl.pallas_call(
        stream_body if streamed else pack_body,
        out_shape=jax.ShapeDtypeStruct((width // NC, BS, SUB, NB), F32),
        in_specs=[pl.BlockSpec(memory_space=pltpu.HBM if streamed else pltpu.VMEM)],
        out_specs=pl.BlockSpec(memory_space=pltpu.VMEM),
        scratch_shapes=scratch,
        compiler_params=pltpu.CompilerParams(vmem_limit_bytes=12 * MIB),
    )(blocks)


def block_product(packed, level, vectors, turned):
    if len(vectors) > BATCH:
        parts = [vectors[i : i + BATCH] for i in range(0, len(vectors), BATCH)]
        return [out for part in parts for out in block_product(packed, level, part, turned)]
    lane = iota((SUB, NB), 1) & (NC - 1)
    totals = [[None] * SUB for _ in vectors]
    for column in range(GROUPS):
        place = lane + ((column + turned) % GROUPS) * NC
        spread = [take_lanes(v, place) for v in vectors]
        for row in range(SUB):
            weight = packed[level, column * SUB + row]
            for total, value in zip(totals, spread):
                piece = weight * value
                total[row] = piece if total[row] is None else total[row] + piece
    return [fold(total) for total in totals]


def turn_step(ops, smooth, level, lows, highs):
    columns = lows + highs
    smoothed = block_product(smooth, level, columns, max(level - 1, 0))
    columns = [pltpu.roll(v, NC, 1) for v in columns]
    rest = [g - a for g, a in zip(columns, block_product(ops, level, smoothed, level))]
    fixed = block_product(smooth, level, rest[: len(lows)], level)
    return rest[len(lows) :], [z + f for z, f in zip(smoothed, fixed)]


def up_step(ops, smooth, level, lows, highs):
    columns = lows + highs
    smoothed = block_product(smooth, level, columns, max(level - 1, 0))
    if level > 0:
        columns = [pltpu.roll(v, NC, 1) for v in columns]
    removed = block_product(ops, level, smoothed[len(lows) :], level)
    saved = list(zip(columns, smoothed[: len(lows)]))
    return saved, [a - b for a, b in zip(columns[len(lows) :], removed)]


def down_step(ops, smooth, level, errors, saved):
    totals = errors
    if saved:
        totals = [pltpu.roll(z, NC, 1) + e for e, (_, z) in zip(errors, saved)]
    applied = block_product(ops, level, totals, level + 1)
    if saved:
        applied = [a - g for a, (g, _) in zip(applied, saved)]
    fixed = block_product(smooth, level, applied, level)
    return [pltpu.roll(t, NB - NC, 1) - f for t, f in zip(totals, fixed)]


def group_sum(load, member, bits):
    start = (member >> bits) << bits
    terms = [load(start + other) for other in range(2**bits)]
    while len(terms) > 1:
        terms = [a + b for a, b in zip(terms[0::2], terms[1::2])]
    return terms[0] * 2.0 ** (-bits / 2)


def near_body(ops, smooth, received, sent, kept):
    count = received.shape[0]
    bits = count.bit_length() - 1
    me = lax.axis_index("plan") & (count - 1)
    across = (((me - 1) ^ 1) + 1) & (count - 1)
    load = lambda n: received[n]
    lows = [load(me), load(me ^ 1), load(across)]
    highs = []
    for level in range(1, bits):
        highs += [group_sum(load, me, level), group_sum(load, across, level)]
    highs.append(group_sum(load, me, bits))
    saved = []
    for level in range(bits - 1):
        pairs, rest = up_step(ops, smooth, level, lows, highs)
        saved.append(pairs)
        lows, highs = rest[:2], rest[2:]
    lows, errors = turn_step(ops, smooth, bits - 1, lows, highs)
    for level in reversed(range(1, bits - 1)):
        errors = down_step(ops, smooth, level, errors, saved[level])
    errors = down_step(ops, smooth, 0, [errors[0], errors[0], errors[1]], saved[0])
    for copy in range(sent.shape[0]):
        sent[copy, 0] = lows[0]
        sent[copy, 1] = errors[2]
    kept[0] = errors[0]
    kept[1] = errors[1]


def far_body(first, ops, smooth, received, near, sent, kept):
    count = received.shape[0]
    bits = count.bit_length() - 1
    members = 2**first
    place = lax.axis_index("plan")
    me, inside = place >> first, place & (members - 1)
    across = me - (inside == 0).astype(jnp.int32) + (inside == members - 1).astype(jnp.int32)
    across = jnp.clip(across, 0, count - 1)
    load = lambda n: received[n, 0]
    lows = [load(me), load(across)]
    highs = []
    for level in range(1, bits):
        highs += [group_sum(load, me, level), group_sum(load, across, level)]
    highs.append(group_sum(load, me, bits))
    saved = []
    for level in range(bits - 1):
        pairs, rest = up_step(ops, smooth, first + level, lows, highs)
        saved.append(pairs)
        lows, highs = rest[:2], rest[2:]
    lows, errors = turn_step(ops, smooth, first + bits - 1, lows, highs)
    for level in reversed(range(bits - 1)):
        errors = down_step(ops, smooth, first + level, errors, saved[level])
    for copy in range(sent.shape[0]):
        sent[copy, 0] = lows[0]
        sent[copy, 1] = near[0]
        sent[copy, 2] = errors[0]
    kept[0] = errors[1]
    kept[1] = received[across, 1]


def top_body(first, middle, ops, smooth, received, near, far, errors, tree):
    count = received.shape[0]
    bits = count.bit_length() - 1
    me, place = lax.axis_index("height"), lax.axis_index("plan")
    last = lax.axis_size("plan") - 1
    targets = (me, jnp.minimum(me + 1, count - 1), jnp.maximum(me - 1, 0))
    values = [received[n, 0] for n in range(count)]
    starts = []
    used = 0
    for level in range(first, LEVELS):
        pairs, _ = up_step(ops, smooth, level, values, [])
        removed = block_product(ops, level, [z for _, z in pairs], level)
        starts.append(used)
        for g, z in pairs:
            tree[used, 0] = g
            tree[used, 1] = z
            used += 1
        rest = [g - r for (g, _), r in zip(pairs, removed)]
        values = [(a + b) * HALF_ROOT for a, b in zip(rest[0::2], rest[1::2])]
    (error,) = block_product(smooth, LEVELS, values, LEVELS - 1)
    parts = [error] * len(targets)
    for level in reversed(range(first, LEVELS)):
        at = [starts[level - first] + (target >> (level - first)) for target in targets]
        saved = [(tree[n, 0], tree[n, 1]) for n in at]
        parts = down_step(ops, smooth, level, parts, saved)
    for level in reversed(range(middle, first)):
        parts = down_step(ops, smooth, level, parts, None)
    parts = [
        parts[0] + received[targets[0], 2],
        parts[0] + far[0],
        parts[1] + received[targets[1], 2],
        parts[2] + received[targets[2], 2],
    ]
    for level in reversed(range(middle)):
        parts = down_step(ops, smooth, level, parts, None)
    zero = jnp.zeros((SUB, NB), F32)
    errors[0] = parts[0] + near[0]
    errors[1] = parts[0] + near[1]
    errors[2] = jnp.where((place > 0) & (place < last), parts[1] + far[1], zero)
    errors[3] = jnp.where(me < count - 1, parts[2] + received[targets[1], 1], zero)
    errors[4] = jnp.where(me > 0, parts[3] + received[targets[2], 1], zero)


def shifted(value, step):
    count = lax.axis_size("height")
    pairs = [(i, i + step) for i in range(count) if 0 <= i + step < count]
    return lax.ppermute(value, "height", pairs)


def swapped(value, first):
    pairs = []
    for low in range(first, lax.axis_size("plan") - 1, 2):
        pairs += [(low, low + 1), (low + 1, low)]
    return lax.ppermute(value, "plan", pairs)


def halo(value):
    inner, outer = swapped(value, 0), swapped(value, 1)
    above, below = shifted(value, -1), shifted(value, 1)
    return inner, outer, above, below


def exchange(value, axis, groups=None):
    return lax.all_to_all(value, axis, 0, 0, axis_index_groups=groups, tiled=True)


def shards(right_side, couplings, neighbours, aggregates, coarse_ops, coarse_smooth):
    source = right_side[0, 0]
    weights = couplings[0, 0]
    links = neighbours[0, 0][:, None, :]
    owners = aggregates[0]
    plan = lax.axis_size("plan")
    height = lax.axis_size("height")
    plan_bits = plan.bit_length() - 1
    low_bits = (plan_bits + 1) // 2
    near = 2**low_bits
    far = plan // near
    field_shape = jax.ShapeDtypeStruct((BS, NB), F32)

    def vectors(*counts):
        return jax.ShapeDtypeStruct((*counts, SUB, NB), F32)

    smooth = pack(coarse_smooth, True)
    around = halo(source)
    smooth, source = lax.optimization_barrier((smooth, source))
    second = call(
        first_body,
        jax.ShapeDtypeStruct((BS + SUB, NB), F32),
        (source, *around, weights, links, owners),
        12 * MIB,
    )
    around = halo(second)
    second, coarse_ops = lax.optimization_barrier((second, coarse_ops))
    ops = pack(coarse_ops, False)
    ops, source = lax.optimization_barrier((ops, source))
    sent = call(
        second_body,
        vectors(near),
        (second, *around, weights, links, source, owners),
        12 * MIB,
        [pltpu.VMEM((BS, NB), F32)],
    )
    near_groups = [[a * near + b for b in range(near)] for a in range(far)]
    far_groups = [[a * near + b for a in range(far)] for b in range(near)]
    received = exchange(sent, "plan", near_groups)
    sent, near_kept = call(
        near_body, (vectors(far, 2), vectors(2)), (ops, smooth, received), 16 * MIB
    )
    received = exchange(sent, "plan", far_groups)
    sent, far_kept = call(
        functools.partial(far_body, low_bits),
        (vectors(height, 3), vectors(2)),
        (ops, smooth, received, near_kept),
        16 * MIB,
    )
    received = exchange(sent, "height")
    errors = call(
        functools.partial(top_body, plan_bits, low_bits),
        vectors(5),
        (ops, smooth, received, near_kept, far_kept),
        16 * MIB,
        [pltpu.VMEM((2 * height, 2, SUB, NB), F32)],
    )
    out = call(
        last_body,
        field_shape,
        (second, *around, errors, weights, links, source),
        12 * MIB,
        [pltpu.VMEM((BS, NB), F32)],
    )
    return out[None, None]


def solution(mesh):
    in_specs = (
        P("plan", "height", None, None),
        P("plan", "height", None, None, None, None),
        P("plan", "height", None, None),
        P("plan", "height", None),
        P(),
        P(),
    )
    out_specs = P("plan", "height", None, None)
    return jax.shard_map(shards, mesh=mesh, in_specs=in_specs, out_specs=out_specs, check_vma=False)
```

```python
import functools
import math

import jax
import jax.numpy as jnp
from jax import lax
from jax.experimental import pallas as pl
from jax.experimental.pallas import tpu as pltpu
from jax.sharding import PartitionSpec as P

BS = 64
NB = 128
NC = 16
LEVELS = 10
SUB = 8
GROUPS = BS // SUB
F32 = jnp.float32
MIB = 1 << 20
HALF_ROOT = 0.7071067811865476
BATCH = 4


def whole(count):
    return [pl.BlockSpec(memory_space=pltpu.VMEM)] * count


def call(body, out_shape, inputs, limit, scratch=()):
    several = isinstance(out_shape, (tuple, list))
    return pl.pallas_call(
        body,
        out_shape=out_shape,
        in_specs=whole(len(inputs)),
        out_specs=whole(len(out_shape)) if several else whole(1)[0],
        scratch_shapes=scratch,
        compiler_params=pltpu.CompilerParams(vmem_limit_bytes=limit),
    )(*inputs)


def iota(shape, axis):
    return lax.broadcasted_iota(jnp.int32, shape, axis)


def fold(rows):
    sub = iota((SUB, NB), 0)
    step = 1
    while len(rows) > 1:
        keep = (sub & step) == 0
        rows = [
            jnp.where(keep, a, b) + pltpu.roll(jnp.where(keep, b, a), step, 0)
            for a, b in zip(rows[0::2], rows[1::2])
        ]
        step *= 2
    return rows[0]


def take_lanes(value, index):
    return jnp.take_along_axis(value, index, axis=1, mode="promise_in_bounds")


def pick(fields, links_ref):
    odd = lax.axis_index("plan") & 1
    numbers = (0, 4 - odd, 2, 3 + odd, 1)
    picked = []
    for which in range(3):
        link = jnp.broadcast_to(links_ref[which], (BS, NB))
        lane, part = link & (NB - 1), link >> 7
        value = take_lanes(fields[0], lane)
        for number, field in zip(numbers[1:], fields[1:]):
            value = jnp.where(part == number, take_lanes(field, lane), value)
        picked.append(value)
    return picked


def coupled(weights_ref, picked, tile):
    rows = []
    for row in range(SUB):
        total = None
        for which in range(3):
            product = weights_ref[which, tile * SUB + row].astype(F32) * picked[which]
            for part in range(GROUPS):
                piece = product[part * SUB : (part + 1) * SUB]
                total = piece if total is None else total + piece
        rows.append(total)
    return fold(rows)


def tiles(step):
    def body(tile, carry):
        step(tile, pl.ds(pl.multiple_of(tile * SUB, SUB), SUB))
        return carry

    lax.fori_loop(0, GROUPS, body, 0)


def first_body(source, inner, above, outer, below, weights, links, owners, second):
    fields = [ref[...] for ref in (source, inner, above, outer, below)]
    picked = pick(fields, links)

    def step(tile, rows):
        mine = source[rows, :]
        applied = 0.5 * (mine + coupled(weights, picked, tile))
        second[rows, :] = 0.5 * mine + 0.5 * (mine - applied)

    tiles(step)
    second[BS:, :] = jnp.broadcast_to(owners[...].astype(F32), (SUB, NB))


def second_body(field, inner, above, outer, below, weights, links, source, owners, sent, left):
    fields = [ref[0:BS, :] for ref in (field, inner, above, outer, below)]
    picked = pick(fields, links)

    def step(tile, rows):
        left[rows, :] = source[rows, :] - (field[rows, :] + coupled(weights, picked, tile))

    tiles(step)
    member = ((iota((NB, NB), 0) & (NC - 1)) == owners[...]).astype(F32)
    spread = lax.dot_general(
        left[...],
        member,
        (((1,), (1,)), ((), ())),
        precision=lax.Precision.HIGHEST,
        preferred_element_type=F32,
    )
    lane_group = iota((SUB, NB), 1) // NC
    packed = spread[0:SUB]
    for group in range(1, GROUPS):
        packed = jnp.where(lane_group == group, spread[group * SUB : (group + 1) * SUB], packed)
    packed = packed * math.sqrt(NC / NB)
    for copy in range(sent.shape[0]):
        sent[copy] = packed


def last_body(field, inner, above, outer, below, errors, weights, links, source, out, third):
    fields = []
    for number, ref in enumerate((field, inner, above, outer, below)):
        error = errors[number]
        owner = ref[BS:, :].astype(jnp.int32)
        added = [take_lanes(error, owner + group * NC) for group in range(GROUPS)]
        fields.append(ref[0:BS, :] + jnp.concatenate(added, axis=0))
    third[...] = fields[0]
    picked = pick(fields, links)

    def step(tile, rows):
        mine = third[rows, :]
        applied = mine + coupled(weights, picked, tile)
        out[rows, :] = mine + 0.5 * (source[rows, :] - applied)

    tiles(step)


def skew(values, count):
    group = iota((SUB, NB), 1) // NC
    values = [v if g == 0 else pltpu.roll(v, NC * g, 1) for g, v in enumerate(values)]
    wanted = [(GROUPS - level) % GROUPS for level in range(count)]
    needed = [set(wanted)]
    for bit in (4, 2):
        needed.append({v for v in needed[-1]} | {(v + bit) % GROUPS for v in needed[-1]})
    for bit, places in zip((1, 2, 4), reversed(needed)):
        second = (group & bit) != 0
        values = [
            jnp.where(second, values[(v + bit) % GROUPS], values[v]) if v in places else None
            for v in range(GROUPS)
        ]
    return [values[v] for v in wanted]


def pack_rows(inner, load, high, packed):
    count = packed.shape[0]
    for part in range(GROUPS):
        high[part, :, 0 : (count - GROUPS) * NC] = load(part, slice(None), slice(NB, None)).astype(F32)
    for column in range(GROUPS):
        rows = slice(column * SUB, (column + 1) * SUB)
        place = column * SUB + inner
        values = [load(part, rows, slice(0, NB)).astype(F32) for part in range(GROUPS)]
        for level, value in enumerate(skew(values, GROUPS)):
            packed[level, place] = value
        values = [high[part, rows, :] for part in range(GROUPS)]
        for level, value in enumerate(skew(values, count - GROUPS)):
            packed[GROUPS + level, place] = value


def pack_body(source, packed, high):
    def body(inner, carry):
        pack_rows(inner, lambda part, rows, lanes: source[part, inner, rows, lanes], high, packed)
        return carry

    lax.fori_loop(0, SUB, body, 0)


def stream_body(source, packed, high, held, sems):
    def copy(inner):
        return pltpu.make_async_copy(source.at[:, inner], held.at[inner], sems.at[inner])

    for inner in range(SUB):
        copy(inner).start()

    def body(inner, carry):
        copy(inner).wait()
        pack_rows(inner, lambda part, rows, lanes: held[inner, part, rows, lanes], high, packed)
        return carry

    lax.fori_loop(0, SUB, body, 0)


def pack(blocks, streamed):
    width = blocks.shape[2]
    blocks = blocks.reshape(GROUPS, SUB, BS, width)
    scratch = [pltpu.VMEM((GROUPS, BS, NB), F32)]
    if streamed:
        blocks = pltpu.with_memory_space_constraint(blocks, pltpu.HBM)
        scratch += [
            pltpu.VMEM((SUB, GROUPS, BS, width), blocks.dtype),
            pltpu.SemaphoreType.DMA((SUB,)),
        ]
    return pl.pallas_call(
        stream_body if streamed else pack_body,
        out_shape=jax.ShapeDtypeStruct((width // NC, BS, SUB, NB), F32),
        in_specs=[pl.BlockSpec(memory_space=pltpu.HBM if streamed else pltpu.VMEM)],
        out_specs=pl.BlockSpec(memory_space=pltpu.VMEM),
        scratch_shapes=scratch,
        compiler_params=pltpu.CompilerParams(vmem_limit_bytes=12 * MIB),
    )(blocks)


def block_product(packed, level, vectors, turned):
    if len(vectors) > BATCH:
        parts = [vectors[i : i + BATCH] for i in range(0, len(vectors), BATCH)]
        return [out for part in parts for out in block_product(packed, level, part, turned)]
    lane = iota((SUB, NB), 1) & (NC - 1)
    totals = [[None] * SUB for _ in vectors]
    for column in range(GROUPS):
        place = lane + ((column + turned) % GROUPS) * NC
        spread = [take_lanes(v, place) for v in vectors]
        for row in range(SUB):
            weight = packed[level, column * SUB + row]
            for total, value in zip(totals, spread):
                piece = weight * value
                total[row] = piece if total[row] is None else total[row] + piece
    return [fold(total) for total in totals]


def up_step(ops, smooth, level, lows, highs):
    columns = lows + highs
    smoothed = block_product(smooth, level, columns, max(level - 1, 0))
    if level > 0:
        columns = [pltpu.roll(v, NC, 1) for v in columns]
    removed = block_product(ops, level, smoothed[len(lows) :], level)
    saved = list(zip(columns, smoothed[: len(lows)]))
    return saved, [a - b for a, b in zip(columns[len(lows) :], removed)]


def down_step(ops, smooth, level, errors, saved):
    totals = []
    for number, error in enumerate(errors):
        total = pltpu.roll(saved[number][1], NC, 1) if saved else error
        totals.append(total if error is None or not saved else total + error)
    applied = block_product(ops, level, totals, level + 1)
    if saved:
        applied = [a - g for a, (g, _) in zip(applied, saved)]
    fixed = block_product(smooth, level, applied, level)
    return [pltpu.roll(t, NB - NC, 1) - f for t, f in zip(totals, fixed)]


def group_sum(load, member, bits):
    start = (member >> bits) << bits
    total = load(start)
    for other in range(1, 2**bits):
        total = total + load(start + other)
    return total * 2.0 ** (-bits / 2)


def near_body(ops, smooth, received, sent, kept):
    count = received.shape[0]
    bits = count.bit_length() - 1
    me = lax.axis_index("plan") & (count - 1)
    across = (((me - 1) ^ 1) + 1) & (count - 1)
    load = lambda n: received[n]
    lows = [load(me), load(me ^ 1), load(across)]
    highs = []
    for level in range(1, bits):
        highs += [group_sum(load, me, level), group_sum(load, across, level)]
    highs.append(group_sum(load, me, bits))
    saved = []
    for level in range(bits):
        pairs, rest = up_step(ops, smooth, level, lows, highs)
        saved.append(pairs)
        lows, highs = rest[:2], rest[2:]
    errors = [None, None]
    for level in reversed(range(1, bits)):
        errors = down_step(ops, smooth, level, errors, saved[level])
    errors = down_step(ops, smooth, 0, [errors[0], errors[0], errors[1]], saved[0])
    for copy in range(sent.shape[0]):
        sent[copy, 0] = lows[0]
        sent[copy, 1] = errors[2]
    kept[0] = errors[0]
    kept[1] = errors[1]


def far_body(first, ops, smooth, received, near, sent, kept):
    count = received.shape[0]
    bits = count.bit_length() - 1
    members = 2**first
    place = lax.axis_index("plan")
    me, inside = place >> first, place & (members - 1)
    across = me - (inside == 0).astype(jnp.int32) + (inside == members - 1).astype(jnp.int32)
    across = jnp.clip(across, 0, count - 1)
    load = lambda n: received[n, 0]
    lows = [load(me), load(across)]
    highs = []
    for level in range(1, bits):
        highs += [group_sum(load, me, level), group_sum(load, across, level)]
    highs.append(group_sum(load, me, bits))
    saved = []
    for level in range(bits):
        pairs, rest = up_step(ops, smooth, first + level, lows, highs)
        saved.append(pairs)
        lows, highs = rest[:2], rest[2:]
    errors = [None, None]
    for level in reversed(range(bits)):
        errors = down_step(ops, smooth, first + level, errors, saved[level])
    for copy in range(sent.shape[0]):
        sent[copy, 0] = lows[0]
        sent[copy, 1] = near[0]
        sent[copy, 2] = errors[0]
    kept[0] = errors[1]
    kept[1] = received[across, 1]


def top_body(first, middle, ops, smooth, received, near, far, errors, tree):
    count = received.shape[0]
    bits = count.bit_length() - 1
    me, place = lax.axis_index("height"), lax.axis_index("plan")
    last = lax.axis_size("plan") - 1
    targets = (me, jnp.minimum(me + 1, count - 1), jnp.maximum(me - 1, 0))
    values = [received[n, 0] for n in range(count)]
    starts = []
    used = 0
    for level in range(first, LEVELS):
        pairs, _ = up_step(ops, smooth, level, values, [])
        removed = block_product(ops, level, [z for _, z in pairs], level)
        starts.append(used)
        for g, z in pairs:
            tree[used, 0] = g
            tree[used, 1] = z
            used += 1
        rest = [g - r for (g, _), r in zip(pairs, removed)]
        values = [(a + b) * HALF_ROOT for a, b in zip(rest[0::2], rest[1::2])]
    (error,) = block_product(smooth, LEVELS, values, LEVELS - 1)
    parts = [error] * len(targets)
    for level in reversed(range(first, LEVELS)):
        at = [starts[level - first] + (target >> (level - first)) for target in targets]
        saved = [(tree[n, 0], tree[n, 1]) for n in at]
        parts = down_step(ops, smooth, level, parts, saved)
    for level in reversed(range(middle, first)):
        parts = down_step(ops, smooth, level, parts, None)
    parts = [
        parts[0] + received[targets[0], 2],
        parts[0] + far[0],
        parts[1] + received[targets[1], 2],
        parts[2] + received[targets[2], 2],
    ]
    for level in reversed(range(middle)):
        parts = down_step(ops, smooth, level, parts, None)
    zero = jnp.zeros((SUB, NB), F32)
    errors[0] = parts[0] + near[0]
    errors[1] = parts[0] + near[1]
    errors[3] = jnp.where((place > 0) & (place < last), parts[1] + far[1], zero)
    errors[2] = jnp.where(me < count - 1, parts[2] + received[targets[1], 1], zero)
    errors[4] = jnp.where(me > 0, parts[3] + received[targets[2], 1], zero)


def shifted(value, step):
    count = lax.axis_size("height")
    pairs = [(i, i + step) for i in range(count) if 0 <= i + step < count]
    return lax.ppermute(value, "height", pairs)


def swapped(value, first):
    pairs = []
    for low in range(first, lax.axis_size("plan") - 1, 2):
        pairs += [(low, low + 1), (low + 1, low)]
    return lax.ppermute(value, "plan", pairs)


def halo(value):
    inner, outer = swapped(value, 0), swapped(value, 1)
    above, below = shifted(value, -1), shifted(value, 1)
    return inner, above, outer, below


def exchange(value, axis, groups=None):
    return lax.all_to_all(value, axis, 0, 0, axis_index_groups=groups, tiled=True)


def shards(right_side, couplings, neighbours, aggregates, coarse_ops, coarse_smooth):
    source = right_side[0, 0]
    weights = couplings[0, 0]
    links = neighbours[0, 0][:, None, :]
    owners = aggregates[0]
    plan = lax.axis_size("plan")
    height = lax.axis_size("height")
    plan_bits = plan.bit_length() - 1
    low_bits = (plan_bits + 1) // 2
    near = 2**low_bits
    far = plan // near
    field_shape = jax.ShapeDtypeStruct((BS, NB), F32)

    def vectors(*counts):
        return jax.ShapeDtypeStruct((*counts, SUB, NB), F32)

    smooth = pack(coarse_smooth, True)
    around = halo(source)
    smooth, source = lax.optimization_barrier((smooth, source))
    second = call(
        first_body,
        jax.ShapeDtypeStruct((BS + SUB, NB), F32),
        (source, *around, weights, links, owners),
        12 * MIB,
    )
    around = halo(second)
    second, coarse_ops = lax.optimization_barrier((second, coarse_ops))
    ops = pack(coarse_ops, False)
    ops, source = lax.optimization_barrier((ops, source))
    sent = call(
        second_body,
        vectors(near),
        (second, *around, weights, links, source, owners),
        12 * MIB,
        [pltpu.VMEM((BS, NB), F32)],
    )
    near_groups = [[a * near + b for b in range(near)] for a in range(far)]
    far_groups = [[a * near + b for a in range(far)] for b in range(near)]
    received = exchange(sent, "plan", near_groups)
    sent, near_kept = call(
        near_body, (vectors(far, 2), vectors(2)), (ops, smooth, received), 16 * MIB
    )
    received = exchange(sent, "plan", far_groups)
    sent, far_kept = call(
        functools.partial(far_body, low_bits),
        (vectors(height, 3), vectors(2)),
        (ops, smooth, received, near_kept),
        16 * MIB,
    )
    received = exchange(sent, "height")
    errors = call(
        functools.partial(top_body, plan_bits, low_bits),
        vectors(5),
        (ops, smooth, received, near_kept, far_kept),
        16 * MIB,
        [pltpu.VMEM((2 * height, 2, SUB, NB), F32)],
    )
    out = call(
        last_body,
        field_shape,
        (second, *around, errors, weights, links, source),
        12 * MIB,
        [pltpu.VMEM((BS, NB), F32)],
    )
    return out[None, None]


def solution(mesh):
    in_specs = (
        P("plan", "height", None, None),
        P("plan", "height", None, None, None, None),
        P("plan", "height", None, None),
        P("plan", "height", None),
        P(),
        P(),
    )
    out_specs = P("plan", "height", None, None)
    return jax.shard_map(shards, mesh=mesh, in_specs=in_specs, out_specs=out_specs, check_vma=False)
```

```python
import functools
import math

import jax
import jax.numpy as jnp
from jax import lax
from jax.experimental import pallas as pl
from jax.experimental.pallas import tpu as pltpu
from jax.sharding import PartitionSpec as P

BS = 64
NB = 128
NC = 16
LEVELS = 10
SUB = 8
GROUPS = BS // SUB
F32 = jnp.float32
MIB = 1 << 20
HALF_ROOT = 0.7071067811865476
BATCH = 4


def whole(count):
    return [pl.BlockSpec(memory_space=pltpu.VMEM)] * count


def call(body, out_shape, inputs, limit, scratch=()):
    several = isinstance(out_shape, (tuple, list))
    return pl.pallas_call(
        body,
        out_shape=out_shape,
        in_specs=whole(len(inputs)),
        out_specs=whole(len(out_shape)) if several else whole(1)[0],
        scratch_shapes=scratch,
        compiler_params=pltpu.CompilerParams(vmem_limit_bytes=limit),
    )(*inputs)


def iota(shape, axis):
    return lax.broadcasted_iota(jnp.int32, shape, axis)


def fold(rows):
    sub = iota((SUB, NB), 0)
    step = 1
    while len(rows) > 1:
        keep = (sub & step) == 0
        rows = [
            jnp.where(keep, a, b) + pltpu.roll(jnp.where(keep, b, a), step, 0)
            for a, b in zip(rows[0::2], rows[1::2])
        ]
        step *= 2
    return rows[0]


def take_lanes(value, index):
    return jnp.take_along_axis(value, index, axis=1, mode="promise_in_bounds")


def pick(fields, links_ref):
    odd = lax.axis_index("plan") & 1
    numbers = (0, 4 - odd, 3 + odd, 1, 2)
    picked = []
    for which in range(3):
        link = jnp.broadcast_to(links_ref[which], (BS, NB))
        lane, part = link & (NB - 1), link >> 7
        value = take_lanes(fields[0], lane)
        for number, field in zip(numbers[1:], fields[1:]):
            value = jnp.where(part == number, take_lanes(field, lane), value)
        picked.append(value)
    return picked


def coupled(weights_ref, picked, tile):
    rows = []
    for row in range(SUB):
        total = None
        for which in range(3):
            product = weights_ref[which, tile * SUB + row].astype(F32) * picked[which]
            for part in range(GROUPS):
                piece = product[part * SUB : (part + 1) * SUB]
                total = piece if total is None else total + piece
        rows.append(total)
    return fold(rows)


def tiles(step):
    def body(tile, carry):
        step(tile, pl.ds(pl.multiple_of(tile * SUB, SUB), SUB))
        return carry

    lax.fori_loop(0, GROUPS, body, 0)


def first_body(source, inner, outer, below, above, weights, links, owners, second):
    fields = [ref[...] for ref in (source, inner, outer, below, above)]
    picked = pick(fields, links)

    def step(tile, rows):
        mine = source[rows, :]
        applied = 0.5 * (mine + coupled(weights, picked, tile))
        second[rows, :] = 0.5 * mine + 0.5 * (mine - applied)

    tiles(step)
    second[BS:, :] = jnp.broadcast_to(owners[...].astype(F32), (SUB, NB))


def second_body(field, inner, outer, below, above, weights, links, source, owners, sent, left):
    fields = [ref[0:BS, :] for ref in (field, inner, outer, below, above)]
    picked = pick(fields, links)

    def step(tile, rows):
        left[rows, :] = source[rows, :] - (field[rows, :] + coupled(weights, picked, tile))

    tiles(step)
    member = ((iota((NB, NB), 0) & (NC - 1)) == owners[...]).astype(F32)
    spread = lax.dot_general(
        left[...],
        member,
        (((1,), (1,)), ((), ())),
        precision=lax.Precision.HIGHEST,
        preferred_element_type=F32,
    )
    lane_group = iota((SUB, NB), 1) // NC
    packed = spread[0:SUB]
    for group in range(1, GROUPS):
        packed = jnp.where(lane_group == group, spread[group * SUB : (group + 1) * SUB], packed)
    packed = packed * math.sqrt(NC / NB)
    for copy in range(sent.shape[0]):
        sent[copy] = packed


def last_body(field, inner, outer, below, above, errors, weights, links, source, out, third):
    fields = []
    for number, ref in enumerate((field, inner, outer, below, above)):
        error = errors[number]
        owner = ref[BS:, :].astype(jnp.int32)
        added = [take_lanes(error, owner + group * NC) for group in range(GROUPS)]
        fields.append(ref[0:BS, :] + jnp.concatenate(added, axis=0))
    third[...] = fields[0]
    picked = pick(fields, links)

    def step(tile, rows):
        mine = third[rows, :]
        applied = mine + coupled(weights, picked, tile)
        out[rows, :] = mine + 0.5 * (source[rows, :] - applied)

    tiles(step)


def skew(values, count):
    group = iota((SUB, NB), 1) // NC
    values = [v if g == 0 else pltpu.roll(v, NC * g, 1) for g, v in enumerate(values)]
    wanted = [(GROUPS - level) % GROUPS for level in range(count)]
    needed = [set(wanted)]
    for bit in (4, 2):
        needed.append({v for v in needed[-1]} | {(v + bit) % GROUPS for v in needed[-1]})
    for bit, places in zip((1, 2, 4), reversed(needed)):
        second = (group & bit) != 0
        values = [
            jnp.where(second, values[(v + bit) % GROUPS], values[v]) if v in places else None
            for v in range(GROUPS)
        ]
    return [values[v] for v in wanted]


def pack_rows(inner, load, high, packed):
    count = packed.shape[0]
    for part in range(GROUPS):
        high[part, :, 0 : (count - GROUPS) * NC] = load(part, slice(None), slice(NB, None)).astype(F32)
    for column in range(GROUPS):
        rows = slice(column * SUB, (column + 1) * SUB)
        place = column * SUB + inner
        values = [load(part, rows, slice(0, NB)).astype(F32) for part in range(GROUPS)]
        for level, value in enumerate(skew(values, GROUPS)):
            packed[level, place] = value
        values = [high[part, rows, :] for part in range(GROUPS)]
        for level, value in enumerate(skew(values, count - GROUPS)):
            packed[GROUPS + level, place] = value


def pack_body(source, packed, high):
    def body(inner, carry):
        pack_rows(inner, lambda part, rows, lanes: source[part, inner, rows, lanes], high, packed)
        return carry

    lax.fori_loop(0, SUB, body, 0)


def stream_body(source, packed, high, held, sems):
    def copy(inner):
        return pltpu.make_async_copy(source.at[:, inner], held.at[inner], sems.at[inner])

    for inner in range(SUB):
        copy(inner).start()

    def body(inner, carry):
        copy(inner).wait()
        pack_rows(inner, lambda part, rows, lanes: held[inner, part, rows, lanes], high, packed)
        return carry

    lax.fori_loop(0, SUB, body, 0)


def pack(blocks, streamed):
    width = blocks.shape[2]
    blocks = blocks.reshape(GROUPS, SUB, BS, width)
    scratch = [pltpu.VMEM((GROUPS, BS, NB), F32)]
    if streamed:
        blocks = pltpu.with_memory_space_constraint(blocks, pltpu.HBM)
        scratch += [
            pltpu.VMEM((SUB, GROUPS, BS, width), blocks.dtype),
            pltpu.SemaphoreType.DMA((SUB,)),
        ]
    return pl.pallas_call(
        stream_body if streamed else pack_body,
        out_shape=jax.ShapeDtypeStruct((width // NC, BS, SUB, NB), F32),
        in_specs=[pl.BlockSpec(memory_space=pltpu.HBM if streamed else pltpu.VMEM)],
        out_specs=pl.BlockSpec(memory_space=pltpu.VMEM),
        scratch_shapes=scratch,
        compiler_params=pltpu.CompilerParams(vmem_limit_bytes=12 * MIB),
    )(blocks)


def block_product(packed, level, vectors, turned):
    if len(vectors) > BATCH:
        parts = [vectors[i : i + BATCH] for i in range(0, len(vectors), BATCH)]
        return [out for part in parts for out in block_product(packed, level, part, turned)]
    lane = iota((SUB, NB), 1) & (NC - 1)
    totals = [[None] * SUB for _ in vectors]
    for column in range(GROUPS):
        place = lane + ((column + turned) % GROUPS) * NC
        spread = [take_lanes(v, place) for v in vectors]
        for row in range(SUB):
            weight = packed[level, column * SUB + row]
            for total, value in zip(totals, spread):
                piece = weight * value
                total[row] = piece if total[row] is None else total[row] + piece
    return [fold(total) for total in totals]


def turn_step(ops, smooth, level, lows, highs):
    columns = lows + highs
    smoothed = block_product(smooth, level, columns, max(level - 1, 0))
    columns = [pltpu.roll(v, NC, 1) for v in columns]
    rest = [g - a for g, a in zip(columns, block_product(ops, level, smoothed, level))]
    fixed = block_product(smooth, level, rest[: len(lows)], level)
    return rest[len(lows) :], [z + f for z, f in zip(smoothed, fixed)]


def up_step(ops, smooth, level, lows, highs):
    columns = lows + highs
    smoothed = block_product(smooth, level, columns, max(level - 1, 0))
    if level > 0:
        columns = [pltpu.roll(v, NC, 1) for v in columns]
    removed = block_product(ops, level, smoothed[len(lows) :], level)
    saved = list(zip(columns, smoothed[: len(lows)]))
    return saved, [a - b for a, b in zip(columns[len(lows) :], removed)]


def down_step(ops, smooth, level, errors, saved):
    totals = errors
    if saved:
        totals = [pltpu.roll(z, NC, 1) + e for e, (_, z) in zip(errors, saved)]
    applied = block_product(ops, level, totals, level + 1)
    if saved:
        applied = [a - g for a, (g, _) in zip(applied, saved)]
    fixed = block_product(smooth, level, applied, level)
    return [pltpu.roll(t, NB - NC, 1) - f for t, f in zip(totals, fixed)]


def group_sum(load, member, bits):
    start = (member >> bits) << bits
    terms = [load(start + other) for other in range(2**bits)]
    while len(terms) > 1:
        terms = [a + b for a, b in zip(terms[0::2], terms[1::2])]
    return terms[0] * 2.0 ** (-bits / 2)


def near_body(ops, smooth, received, sent, kept):
    count = received.shape[0]
    bits = count.bit_length() - 1
    me = lax.axis_index("plan") & (count - 1)
    across = (((me - 1) ^ 1) + 1) & (count - 1)
    load = lambda n: received[n]
    lows = [load(me), load(me ^ 1), load(across)]
    highs = []
    for level in range(1, bits):
        highs += [group_sum(load, me, level), group_sum(load, across, level)]
    highs.append(group_sum(load, me, bits))
    saved = []
    for level in range(bits - 1):
        pairs, rest = up_step(ops, smooth, level, lows, highs)
        saved.append(pairs)
        lows, highs = rest[:2], rest[2:]
    lows, errors = turn_step(ops, smooth, bits - 1, lows, highs)
    for level in reversed(range(1, bits - 1)):
        errors = down_step(ops, smooth, level, errors, saved[level])
    errors = down_step(ops, smooth, 0, [errors[0], errors[0], errors[1]], saved[0])
    for copy in range(sent.shape[0]):
        sent[copy, 0] = lows[0]
        sent[copy, 1] = errors[2]
    kept[0] = errors[0]
    kept[1] = errors[1]


def far_body(first, ops, smooth, received, near, sent, kept):
    count = received.shape[0]
    bits = count.bit_length() - 1
    members = 2**first
    place = lax.axis_index("plan")
    me, inside = place >> first, place & (members - 1)
    across = me - (inside == 0).astype(jnp.int32) + (inside == members - 1).astype(jnp.int32)
    across = jnp.clip(across, 0, count - 1)
    load = lambda n: received[n, 0]
    lows = [load(me), load(across)]
    highs = []
    for level in range(1, bits):
        highs += [group_sum(load, me, level), group_sum(load, across, level)]
    highs.append(group_sum(load, me, bits))
    saved = []
    for level in range(bits - 1):
        pairs, rest = up_step(ops, smooth, first + level, lows, highs)
        saved.append(pairs)
        lows, highs = rest[:2], rest[2:]
    lows, errors = turn_step(ops, smooth, first + bits - 1, lows, highs)
    for level in reversed(range(bits - 1)):
        errors = down_step(ops, smooth, first + level, errors, saved[level])
    for copy in range(sent.shape[0]):
        sent[copy, 0] = lows[0]
        sent[copy, 1] = near[0]
        sent[copy, 2] = errors[0]
    kept[0] = errors[1]
    kept[1] = received[across, 1]


def top_body(first, middle, ops, smooth, received, near, far, errors, tree):
    count = received.shape[0]
    bits = count.bit_length() - 1
    me, place = lax.axis_index("height"), lax.axis_index("plan")
    last = lax.axis_size("plan") - 1
    targets = (me, jnp.minimum(me + 1, count - 1), jnp.maximum(me - 1, 0))
    values = [received[n, 0] for n in range(count)]
    starts = []
    used = 0
    for level in range(first, LEVELS):
        pairs, _ = up_step(ops, smooth, level, values, [])
        removed = block_product(ops, level, [z for _, z in pairs], level)
        starts.append(used)
        for g, z in pairs:
            tree[used, 0] = g
            tree[used, 1] = z
            used += 1
        rest = [g - r for (g, _), r in zip(pairs, removed)]
        values = [(a + b) * HALF_ROOT for a, b in zip(rest[0::2], rest[1::2])]
    (error,) = block_product(smooth, LEVELS, values, LEVELS - 1)
    parts = [error] * len(targets)
    for level in reversed(range(first, LEVELS)):
        at = [starts[level - first] + (target >> (level - first)) for target in targets]
        saved = [(tree[n, 0], tree[n, 1]) for n in at]
        parts = down_step(ops, smooth, level, parts, saved)
    for level in reversed(range(middle, first)):
        parts = down_step(ops, smooth, level, parts, None)
    parts = [
        parts[0] + received[targets[0], 2],
        parts[0] + far[0],
        parts[1] + received[targets[1], 2],
        parts[2] + received[targets[2], 2],
    ]
    for level in reversed(range(middle)):
        parts = down_step(ops, smooth, level, parts, None)
    zero = jnp.zeros((SUB, NB), F32)
    errors[0] = parts[0] + near[0]
    errors[1] = parts[0] + near[1]
    errors[2] = jnp.where((place > 0) & (place < last), parts[1] + far[1], zero)
    errors[4] = jnp.where(me < count - 1, parts[2] + received[targets[1], 1], zero)
    errors[3] = jnp.where(me > 0, parts[3] + received[targets[2], 1], zero)


def shifted(value, step):
    count = lax.axis_size("height")
    pairs = [(i, i + step) for i in range(count) if 0 <= i + step < count]
    return lax.ppermute(value, "height", pairs)


def swapped(value, first):
    pairs = []
    for low in range(first, lax.axis_size("plan") - 1, 2):
        pairs += [(low, low + 1), (low + 1, low)]
    return lax.ppermute(value, "plan", pairs)


def halo(value):
    inner, outer = swapped(value, 0), swapped(value, 1)
    above, below = shifted(value, -1), shifted(value, 1)
    return inner, outer, below, above


def exchange(value, axis, groups=None):
    return lax.all_to_all(value, axis, 0, 0, axis_index_groups=groups, tiled=True)


def shards(right_side, couplings, neighbours, aggregates, coarse_ops, coarse_smooth):
    source = right_side[0, 0]
    weights = couplings[0, 0]
    links = neighbours[0, 0][:, None, :]
    owners = aggregates[0]
    plan = lax.axis_size("plan")
    height = lax.axis_size("height")
    plan_bits = plan.bit_length() - 1
    low_bits = (plan_bits + 1) // 2
    near = 2**low_bits
    far = plan // near
    field_shape = jax.ShapeDtypeStruct((BS, NB), F32)

    def vectors(*counts):
        return jax.ShapeDtypeStruct((*counts, SUB, NB), F32)

    smooth = pack(coarse_smooth, True)
    around = halo(source)
    smooth, source = lax.optimization_barrier((smooth, source))
    second = call(
        first_body,
        jax.ShapeDtypeStruct((BS + SUB, NB), F32),
        (source, *around, weights, links, owners),
        12 * MIB,
    )
    around = halo(second)
    second, coarse_ops = lax.optimization_barrier((second, coarse_ops))
    ops = pack(coarse_ops, False)
    ops, source = lax.optimization_barrier((ops, source))
    sent = call(
        second_body,
        vectors(near),
        (second, *around, weights, links, source, owners),
        12 * MIB,
        [pltpu.VMEM((BS, NB), F32)],
    )
    near_groups = [[a * near + b for b in range(near)] for a in range(far)]
    far_groups = [[a * near + b for a in range(far)] for b in range(near)]
    received = exchange(sent, "plan", near_groups)
    sent, near_kept = call(
        near_body, (vectors(far, 2), vectors(2)), (ops, smooth, received), 16 * MIB
    )
    received = exchange(sent, "plan", far_groups)
    sent, far_kept = call(
        functools.partial(far_body, low_bits),
        (vectors(height, 3), vectors(2)),
        (ops, smooth, received, near_kept),
        16 * MIB,
    )
    received = exchange(sent, "height")
    errors = call(
        functools.partial(top_body, plan_bits, low_bits),
        vectors(5),
        (ops, smooth, received, near_kept, far_kept),
        16 * MIB,
        [pltpu.VMEM((2 * height, 2, SUB, NB), F32)],
    )
    out = call(
        last_body,
        field_shape,
        (second, *around, errors, weights, links, source),
        12 * MIB,
        [pltpu.VMEM((BS, NB), F32)],
    )
    return out[None, None]


def solution(mesh):
    in_specs = (
        P("plan", "height", None, None),
        P("plan", "height", None, None, None, None),
        P("plan", "height", None, None),
        P("plan", "height", None),
        P(),
        P(),
    )
    out_specs = P("plan", "height", None, None)
    return jax.shard_map(shards, mesh=mesh, in_specs=in_specs, out_specs=out_specs, check_vma=False)
```
